256 devices in a mesh: ctx: 256 (over y, z, x, core).
Axes of the slice: x: 4, y: 4, z: 8, core: 2. Of those that a mesh axis runs over, the one named last changes fastest.
Arguments:
- queries: bfloat16 [65536, 768], P('ctx'), may hold values from -16 to 16
- keys: bfloat16 [65536, 768], P('ctx'), may hold values from -16 to 16
- values: bfloat16 [65536, 768], P('ctx'), may hold values from -6 to 6
- offsets: int32 [5, 12], replicated, may hold values from 0 to 255, as said below
Outputs:
- attended: bfloat16 [65536, 768], P('ctx')
The draws below stay inside these ranges and needn't reach their ends.
Inputs may be any that keep to these rules, and one draw needn't show every extreme that they name: offsets[l, h] lies in 0 to min(4 ** l, 256) - 1.
All inputs are finite; a program needn't handle non-finite values.
Results may differ from the reference program's by a relative error of at most 0.0035.
Values may be sent and summed in bfloat16 or wider, within the bound.
No kernel may reach another device: no remote copies, remote signals or barrier semaphores. Data moves between devices by JAX's collectives and lax.ppermute only.
A program may use at most 64 MiB of HBM per device.

```python
import jax
import jax.numpy as jnp
from jax import lax

HEADS = 12
HEAD_DIM = 64
LEVELS = 5
TOK_DEV = 256
D = 768
SEQ = 65536
N_CTX = 256


def draw_keys(key, part):
    base = jax.random.normal(jax.random.fold_in(key, 11), (SEQ, D), jnp.float32)
    return jnp.clip(base, -16.0, 16.0).astype(jnp.bfloat16)


def draw_queries(key, part):
    base = jax.random.normal(jax.random.fold_in(key, 13), (SEQ, D), jnp.float32)
    return jnp.clip(base, -16.0, 16.0).astype(jnp.bfloat16)


def draw_offsets(key, part):
    spans = jnp.minimum(4 ** jnp.arange(LEVELS, dtype=jnp.int32), N_CTX)
    raw = jax.random.randint(jax.random.fold_in(key, 17), (LEVELS, HEADS), 0, 1 << 20)
    return (raw % spans[:, None]).astype(jnp.int32)


def levels(key, extent, split, smallest, top_value):
    def one(axis_at, shards_of):
        heights = jax.random.uniform(jax.random.fold_in(jax.random.fold_in(key, 6), axis_at), (shards_of,), jnp.float32, smallest / len(split), top_value / len(split))
        return jnp.repeat(jnp.exp(heights), extent[axis_at] // shards_of).reshape((-1,) + (1,) * (len(extent) - axis_at - 1))

    level = one(*split[0])
    for cut in split[1:]:
        level = level * one(*cut)
    return level


def scatter_about(stream_key, dims, spread, most, cuts=(), held_as=jnp.bfloat16):
    drawn = jax.random.normal(stream_key, dims, jnp.float32) * spread
    if len(cuts) > 0:
        drawn = levels(stream_key, dims, cuts, -0.22, 0.18) * drawn
    return jnp.clip(drawn, min=-most, max=most).astype(held_as)


def setup_inputs(seed: int = 0) -> dict:
    seeds = jax.random.split(jax.random.key(seed), 5)
    queries = draw_queries(jax.random.fold_in(seeds[4], 71), 0)
    keys = draw_keys(jax.random.fold_in(seeds[4], 71), 0)
    values = scatter_about(seeds[2], (SEQ, D), 1.0, 6.0, ((0, 256),))
    offsets = draw_offsets(jax.random.fold_in(seeds[4], 71), 0)
    return {"queries": queries, "keys": keys, "values": values, "offsets": offsets}


def attend_rows(query_rows, key_rows, value_rows, query_pos, key_pos, heads, scale):
    rows = query_rows.shape[0]
    cols = key_rows.shape[0]
    head_size = query_rows.shape[1] // heads
    query_heads = query_rows.reshape(rows, heads, head_size)
    key_heads = key_rows.reshape(cols, heads, head_size)
    value_heads = value_rows.reshape(cols, heads, head_size)
    allowed = key_pos[None, :] <= query_pos[:, None]
    scores = jnp.einsum("qhd,khd->hqk", query_heads, key_heads, preferred_element_type=jnp.float32) * scale
    scores = jnp.where(allowed[None], scores, -1e30)
    peak = jnp.max(scores, axis=2)
    weights = jnp.where(allowed[None], jnp.exp(scores - peak[:, :, None]), 0.0)
    totals = jnp.sum(weights, axis=2)
    result = jnp.einsum("hqk,khd->qhd", weights.astype(jnp.bfloat16), value_heads, preferred_element_type=jnp.float32)
    return result / totals.T[:, :, None], (peak + jnp.log(totals)).T


def causal_blocks(query_rows, key_rows, value_rows, heads, scale):
    length = query_rows.shape[0]
    block = min(512, length)
    outputs = []
    sums = []
    for number in range(length // block):
        query_pos = jnp.arange(number * block, (number + 1) * block, dtype=jnp.int32)
        key_pos = jnp.arange((number + 1) * block, dtype=jnp.int32)
        result, lse_part = attend_rows(query_rows[number * block:(number + 1) * block], key_rows[:(number + 1) * block], value_rows[:(number + 1) * block], query_pos, key_pos, heads, scale)
        outputs.append(result)
        sums.append(lse_part)
    return jnp.concatenate(outputs, 0), jnp.concatenate(sums, 0)


def select_rows(source, offset_row, group, heads):
    count = source.shape[0]
    head_size = source.shape[1] // heads
    shaped = source.reshape(count // group, group, heads, head_size)
    hit = jnp.arange(group, dtype=jnp.int32)[:, None] == offset_row.astype(jnp.int32)[None, :]
    picked = jnp.sum(jnp.where(hit[None, :, :, None], shaped, jnp.zeros((), source.dtype)), axis=1)
    return picked.astype(source.dtype).reshape(count // group, heads * head_size)


def merge_levels(base_out, base_lse, extras):
    rows_all, heads, head_size = base_out.shape
    best = base_lse
    numer = base_out
    denom = jnp.ones(base_lse.shape, jnp.float32)
    for level_out, level_lse, offset_row, group in extras:
        rows = level_out.shape[0]
        hit = jnp.arange(group, dtype=jnp.int32)[:, None] == offset_row.astype(jnp.int32)[None, :]
        best_g = best.reshape(rows, group, heads)
        lse_g = jnp.where(hit[None], level_lse[:, None], -1e30)
        newest = jnp.maximum(best_g, lse_g)
        keep_old = jnp.exp(best_g - newest)
        take_new = jnp.exp(lse_g - newest)
        numer = (numer.reshape(rows, group, heads, head_size) * keep_old[..., None] + level_out[:, None] * take_new[..., None]).reshape(rows_all, heads, head_size)
        denom = (denom.reshape(rows, group, heads) * keep_old + take_new).reshape(rows_all, heads)
        best = newest.reshape(rows_all, heads)
    merged = numer / denom[..., None]
    return merged.reshape(rows_all, -1).astype(jnp.bfloat16)


def reference(queries, keys, values, offsets):
    scale = HEAD_DIM ** -0.5
    level_outs = []
    level_lses = []
    for height in range(LEVELS):
        group = min(4 ** height, N_CTX)
        segments = SEQ // (TOK_DEV * group)
        picked_q = select_rows(queries, offsets[height], group, HEADS).reshape(segments, TOK_DEV, D)
        picked_k = select_rows(keys, offsets[height], group, HEADS).reshape(segments, TOK_DEV, D)
        picked_v = select_rows(values, offsets[height], group, HEADS).reshape(segments, TOK_DEV, D)
        outs, lses = lax.map(lambda triple: causal_blocks(triple[0], triple[1], triple[2], HEADS, scale), (picked_q, picked_k, picked_v))
        rows = TOK_DEV // group
        level_outs.append(outs.reshape(N_CTX, rows, HEADS, HEAD_DIM))
        level_lses.append(lses.reshape(N_CTX, rows, HEADS))

    def per_shard(shard_data):
        shard_outs, shard_lses = shard_data
        extras = []
        for height in range(1, LEVELS):
            extras.append((shard_outs[height], shard_lses[height], offsets[height], min(4 ** height, N_CTX)))
        return merge_levels(shard_outs[0], shard_lses[0], extras)

    shards = lax.map(per_shard, (tuple(level_outs), tuple(level_lses)))
    return shards.reshape(SEQ, D)
```

```python
import functools

import jax
import jax.numpy as jnp
from jax import lax
from jax.experimental import pallas as pl
from jax.experimental.pallas import tpu as pltpu
from jax.sharding import PartitionSpec as P

HEADS = 12
PAIRS = 6
LANES = 128
HALF = 64
TOK = 256
WIDTH = 768
NEG = -1e30
SCALE = 0.125
F32 = jnp.float32
BF16 = jnp.bfloat16
SEL = 96
STAT = 16
VMEM = pl.BlockSpec(memory_space=pltpu.VMEM)
SMEM = pl.BlockSpec(memory_space=pltpu.SMEM)


def iota(shape, dim):
    return lax.broadcasted_iota(jnp.int32, shape, dim)


def dot_nt(a, b):
    return lax.dot_general(a, b, (((1,), (1,)), ((), ())), preferred_element_type=F32)


def dot_nn(a, b):
    return jnp.dot(a, b, preferred_element_type=F32)


def lanes_of(pair):
    return slice(pair * LANES, (pair + 1) * LANES)


def split_heads(rows):
    low = iota(rows.shape, 1) < HALF
    zero = jnp.zeros_like(rows)
    return jnp.concatenate([jnp.where(low, rows, zero), jnp.where(low, zero, rows)], 0)


def join_heads(stacked):
    n = stacked.shape[0] // 2
    low = iota((n, LANES), 1) < HALF
    return jnp.where(low, stacked[:n], stacked[n:])


def put_stats(stats, pair, peak, total):
    n = stats.shape[0]
    lane = iota(stats.shape, 1)
    for side in range(2):
        head = 2 * pair + side
        stats = jnp.where(lane == head, peak[side * n:(side + 1) * n], stats)
        stats = jnp.where(lane == STAT + head, total[side * n:(side + 1) * n], stats)
    return stats


def call(body, outs, n_smem, n_in, flops, nbytes):
    return pl.pallas_call(
        body,
        out_shape=outs,
        in_specs=[SMEM] * n_smem + [VMEM] * (n_in - n_smem),
        out_specs=[VMEM] * len(outs),
        cost_estimate=pl.CostEstimate(flops=flops, bytes_accessed=nbytes, transcendentals=0),
    )


def select_kernel(off_ref, q_ref, k_ref, v_ref, q1_ref, q2_ref, q34_ref, kv1_ref, kv2_ref, kv34_ref):
    row = iota((SEL, TOK), 0)
    tok = iota((SEL, TOK), 1)
    base = jnp.where(row < 64, row * 4, jnp.where(row < 80, (row - 64) * 16, (row - 80) * 64))
    base = jnp.where(row < 84, base, 0)
    for pair in range(PAIRS):
        picks = []
        for side in range(2):
            head = 2 * pair + side
            off = jnp.where(
                row < 64,
                off_ref[1, head],
                jnp.where(row < 80, off_ref[2, head], jnp.where(row < 84, off_ref[3, head], off_ref[4, head])),
            )
            hit = (tok == base + off) & (row < 85)
            picks.append(jnp.where(hit, 1.0, 0.0).astype(BF16))
        pick = jnp.concatenate(picks, 0)
        at = lanes_of(pair)
        rows = join_heads(dot_nn(pick, q_ref[:, at]) * SCALE).astype(BF16)
        q1_ref[:, at] = rows[0:64]
        q2_ref[:, at] = rows[64:80]
        q34_ref[:, at] = rows[80:88]
        for part, ref in enumerate((k_ref, v_ref)):
            rows = join_heads(dot_nn(pick, ref[:, at])).astype(BF16)
            here = slice(part * WIDTH + pair * LANES, part * WIDTH + (pair + 1) * LANES)
            kv1_ref[:, here] = rows[0:64]
            kv2_ref[:, here] = rows[64:80]
            kv34_ref[:, here] = rows[80:88]


def local_kernel(q_ref, k_ref, v_ref, acc_ref, stat_ref):
    half = TOK // 2
    for part in range(2):
        keys = (part + 1) * half
        here = slice(part * half, keys)
        query = iota((2 * half, keys), 0) % half + part * half
        allowed = iota((2 * half, keys), 1) <= query
        stats = jnp.zeros((half, LANES), F32)
        for pair in range(PAIRS):
            at = lanes_of(pair)
            queries = split_heads(q_ref[here, at] * jnp.asarray(SCALE, BF16))
            scores = jnp.where(allowed, dot_nt(queries, k_ref[0:keys, at]), NEG)
            peak = jnp.max(scores, axis=1, keepdims=True)
            weights = jnp.exp(scores - peak)
            total = jnp.sum(weights, axis=1, keepdims=True)
            acc_ref[here, at] = join_heads(dot_nn(weights.astype(BF16), v_ref[0:keys, at]))
            stats = put_stats(stats, pair, peak, total)
        stat_ref[here, :] = stats


def gathered(q_ref, kv_refs, q_pos, k_pos, acc_ref, stat_ref, first, rows):
    allowed = k_pos <= q_pos
    stats = jnp.zeros((rows, LANES), F32)
    for pair in range(PAIRS):
        at = lanes_of(pair)
        vat = slice(WIDTH + pair * LANES, WIDTH + (pair + 1) * LANES)
        queries = split_heads(q_ref[:, at])
        scores = jnp.concatenate([dot_nt(queries, ref[:, at]) for ref in kv_refs], 1)
        scores = jnp.where(allowed, scores, NEG)
        peak = jnp.max(scores, axis=1, keepdims=True)
        weights = jnp.exp(scores - peak)
        total = jnp.sum(weights, axis=1, keepdims=True)
        weights = weights.astype(BF16)
        acc = dot_nn(weights[:, 0:128], kv_refs[0][:, vat]) + dot_nn(weights[:, 128:256], kv_refs[1][:, vat])
        acc_ref[first:first + rows, at] = join_heads(acc)
        stats = put_stats(stats, pair, peak, total)
    stat_ref[first:first + rows, :] = stats


def near_kernel(pos_ref, q1_ref, q2_ref, a1_ref, b1_ref, a2_ref, b2_ref, acc_ref, stat_ref):
    me = pos_ref[0]
    col = iota((128, TOK), 1)
    device = me ^ (((col >> 6) & 1) * 2 + (col >> 7))
    k_pos = (device & 3) * 64 + (col & 63)
    q_pos = (me & 3) * 64 + (iota((128, TOK), 0) & 63)
    gathered(q1_ref, (a1_ref, b1_ref), q_pos, k_pos, acc_ref, stat_ref, 0, 64)
    col = iota((32, TOK), 1)
    device = me ^ (((col >> 4) & 7) * 2 + (col >> 7))
    k_pos = (device & 15) * 16 + (col & 15)
    q_pos = (me & 15) * 16 + (iota((32, TOK), 0) & 15)
    gathered(q2_ref, (a2_ref, b2_ref), q_pos, k_pos, acc_ref, stat_ref, 64, 16)


def far_kernel(pos_ref, q_ref, kv_ref, out_ref):
    me = pos_ref[0]
    row = iota((128, 64), 0) & 63
    asker = me ^ (row >> 3)
    q_row = row & 7
    col = iota((128, 64), 1)
    k_row = col & 7
    group = col >> 3
    owner = me ^ ((group & 1) * 32 + ((group >> 1) & 1) * 16 + ((group >> 2) & 1) * 8)
    far_owner = owner ^ ((k_row & 1) * 128 + ((k_row >> 1) & 1) * 64)
    third = (k_row < 4) & (q_row < 4) & ((owner & 63) * 4 + k_row <= (asker & 63) * 4 + q_row)
    fourth = (k_row >= 4) & (q_row == 4) & (far_owner <= asker)
    allowed = third | fourth
    stats = jnp.zeros((64, LANES), F32)
    accs = []
    for pair in range(PAIRS):
        at = lanes_of(pair)
        vat = slice(WIDTH + pair * LANES, WIDTH + (pair + 1) * LANES)
        scores = jnp.where(allowed, dot_nt(split_heads(q_ref[:, at]), kv_ref[:, at]), NEG)
        peak = jnp.max(scores, axis=1, keepdims=True)
        weights = jnp.where(allowed, jnp.exp(scores - peak), 0.0)
        total = jnp.sum(weights, axis=1, keepdims=True)
        accs.append(join_heads(dot_nn(weights.astype(BF16), kv_ref[:, vat])))
        stats = put_stats(stats, pair, peak, total)
    for number in range(8):
        to = pl.ds(pl.multiple_of((number ^ (me & 7)) * 8, 8), 8)
        for pair in range(PAIRS):
            out_ref[to, lanes_of(pair)] = accs[pair][number * 8:(number + 1) * 8]
        out_ref[to, WIDTH:WIDTH + LANES] = stats[number * 8:(number + 1) * 8]


def split2(value):
    high = value.astype(BF16)
    return high, (value - high.astype(F32)).astype(BF16)


def over_lanes(coeff):
    high, low = split2(coeff)
    lane = iota((2 * LANES, WIDTH), 1) // HALF
    spread = jnp.where((iota((2 * LANES, WIDTH), 0) & (LANES - 1)) == lane, 1.0, 0.0).astype(BF16)
    return dot_nn(jnp.concatenate([high, low], 1), spread)


def final_kernel(off_ref, acc0_ref, stat0_ref, acc12_ref, stat12_ref, ret_ref, out_ref):
    lane8 = iota((8, LANES), 1)
    parts = [ret_ref[8 * n:8 * n + 8, :] for n in range(8)]
    part_stats = [part[:, WIDTH:] for part in parts]
    peaks = [jnp.where(lane8 < HEADS, part, NEG) for part in part_stats]
    peak34 = functools.reduce(jnp.maximum, peaks)
    factors = [jnp.where(lane8 < HEADS, jnp.exp(peak - peak34), 0.0) for peak in peaks]
    totals = [pltpu.roll(part, LANES - STAT, 1) for part in part_stats]
    total34 = sum(f * t for f, t in zip(factors, totals))
    spread = over_lanes(jnp.concatenate(factors, 0))
    acc34 = sum(spread[8 * n:8 * n + 8] * parts[n][:, 0:WIDTH] for n in range(8))

    def expander(group, rows, first):
        tok = iota((TOK, rows), 0)
        return jnp.where(tok // group == iota((TOK, rows), 1) - first, 1.0, 0.0)

    lane = iota((TOK, LANES), 1)
    tok = iota((TOK, LANES), 0)
    stat12 = stat12_ref[...]
    stat_rows = [(stat12[0:64, :], pltpu.roll(stat12[0:64, :], LANES - STAT, 1)),
                 (stat12[64:80, :], pltpu.roll(stat12[64:80, :], LANES - STAT, 1)),
                 (peak34, total34),
                 (peak34, total34)]
    acc_rows = [acc12_ref[0:64, :], acc12_ref[64:80, :], acc34, acc34]
    firsts = [0, 0, 0, 4]
    stat0 = stat0_ref[...]
    level_peaks = [jnp.where(lane < HEADS, stat0, 0.0)]
    level_totals = [pltpu.roll(stat0, LANES - STAT, 1)]
    expanders = []
    for level in range(1, 5):
        group = 4**level
        rows = stat_rows[level - 1][0].shape[0]
        expand = expander(group, rows, firsts[level - 1])
        expanders.append(expand.astype(BF16))
        off = jnp.zeros((TOK, LANES), jnp.int32)
        for head in range(HEADS):
            off = jnp.where(lane == head, off_ref[level, head], off)
        kept = ((tok & (group - 1)) == off) & (lane < HEADS)
        peak = jnp.dot(expand, stat_rows[level - 1][0], precision=lax.Precision.HIGHEST, preferred_element_type=F32)
        total = jnp.dot(expand, stat_rows[level - 1][1], precision=lax.Precision.HIGHEST, preferred_element_type=F32)
        level_peaks.append(jnp.where(kept, peak, NEG))
        level_totals.append(total)
    best = functools.reduce(jnp.maximum, level_peaks)
    shares = [jnp.exp(peak - best) for peak in level_peaks]
    shares = [jnp.where(lane < HEADS, share, 0.0) for share in shares]
    denom = sum(share * total for share, total in zip(shares, level_totals))
    denom = jnp.where(lane < HEADS, denom, 1.0)
    shares = [share / denom for share in shares]
    merged = over_lanes(shares[0]) * acc0_ref[...]
    for level in range(1, 5):
        high, low = split2(acc_rows[level - 1])
        expand = jnp.concatenate([expanders[level - 1]] * 2, 1)
        rows = dot_nn(expand, jnp.concatenate([high, low], 0))
        merged = merged + over_lanes(shares[level]) * rows
    out_ref[...] = merged.astype(BF16)


def shaped(rows, width, dtype):
    return jax.ShapeDtypeStruct((rows, width), dtype)


def traded(value, mask, count):
    return lax.ppermute(value, "ctx", [(source, source ^ mask) for source in range(count)])


def grown(value, mask, count):
    return jnp.concatenate([value, traded(value, mask, count)], 0)


def body(queries, keys, values, offsets):
    count = lax.axis_size("ctx")
    me = lax.axis_index("ctx").astype(jnp.int32).reshape(1)
    q1, q2, q34, kv1, kv2, kv34 = call(
        select_kernel,
        [shaped(64, WIDTH, BF16), shaped(16, WIDTH, BF16), shaped(8, WIDTH, BF16),
         shaped(64, 2 * WIDTH, BF16), shaped(16, 2 * WIDTH, BF16), shaped(8, 2 * WIDTH, BF16)],
        1, 4, 200_000_000, 2_000_000,
    )(offsets, queries, keys, values)
    far = kv34[4:5]
    for mask in (128, 64):
        far = grown(far, mask, count)
    far = jnp.concatenate([kv34[0:4], far], 0)
    for mask in (32, 16, 8):
        far = grown(far, mask, count)
    asked = q34
    for mask in (1, 2, 4):
        asked = grown(asked, mask, count)
    kv1 = grown(kv1, 2, count)
    kv1_other = traded(kv1, 1, count)
    for mask in (2, 4, 8):
        kv2 = grown(kv2, mask, count)
    kv2_other = traded(kv2, 1, count)
    acc0, stat0 = call(
        local_kernel, [shaped(TOK, WIDTH, F32), shaped(TOK, LANES, F32)], 0, 3, 1_000_000_000, 3_000_000
    )(queries, keys, values)
    acc12, stat12 = call(
        near_kernel, [shaped(80, WIDTH, F32), shaped(80, LANES, F32)], 1, 7, 600_000_000, 2_000_000
    )(me, q1, q2, kv1, kv1_other, kv2, kv2_other)
    (partial,) = call(far_kernel, [shaped(64, WIDTH + LANES, F32)], 1, 3, 200_000_000, 600_000)(me, asked, far)
    groups = [list(range(first, first + 8)) for first in range(0, count, 8)]
    back = lax.all_to_all(partial.reshape(8, 8, WIDTH + LANES), "ctx", 0, 0, axis_index_groups=groups)
    (merged,) = call(final_kernel, [shaped(TOK, WIDTH, BF16)], 1, 6, 1_000_000_000, 3_000_000)(
        offsets, acc0, stat0, acc12, stat12, back.reshape(64, WIDTH + LANES)
    )
    return merged


def solution(mesh):
    in_specs = (P("ctx", None), P("ctx", None), P("ctx", None), P())
    return jax.shard_map(body, mesh=mesh, in_specs=in_specs, out_specs=P("ctx", None), check_vma=False)
```

```python
import functools

import jax
import jax.numpy as jnp
from jax import lax
from jax.experimental import pallas as pl
from jax.experimental.pallas import tpu as pltpu
from jax.sharding import PartitionSpec as P

HEADS = 12
PAIRS = 6
LANES = 128
HALF = 64
TOK = 256
WIDTH = 768
NEG = -1e30
SCALE = 0.125
F32 = jnp.float32
BF16 = jnp.bfloat16
SEL = 96
STAT = 16
VMEM = pl.BlockSpec(memory_space=pltpu.VMEM)
SMEM = pl.BlockSpec(memory_space=pltpu.SMEM)


def iota(shape, dim):
    return lax.broadcasted_iota(jnp.int32, shape, dim)


def dot_nt(a, b):
    return lax.dot_general(a, b, (((1,), (1,)), ((), ())), preferred_element_type=F32)


def dot_nn(a, b):
    return jnp.dot(a, b, preferred_element_type=F32)


def lanes_of(pair):
    return slice(pair * LANES, (pair + 1) * LANES)


def split_heads(rows):
    low = iota(rows.shape, 1) < HALF
    zero = jnp.zeros_like(rows)
    return jnp.concatenate([jnp.where(low, rows, zero), jnp.where(low, zero, rows)], 0)


def join_heads(stacked):
    n = stacked.shape[0] // 2
    low = iota((n, LANES), 1) < HALF
    return jnp.where(low, stacked[:n], stacked[n:])


def put_stats(stats, pair, peak, total):
    n = stats.shape[0]
    lane = iota(stats.shape, 1)
    for side in range(2):
        head = 2 * pair + side
        stats = jnp.where(lane == head, peak[side * n:(side + 1) * n], stats)
        stats = jnp.where(lane == STAT + head, total[side * n:(side + 1) * n], stats)
    return stats


def call(body, outs, in_specs, flops, nbytes, grant):
    return pl.pallas_call(
        body,
        compiler_params=pltpu.CompilerParams(vmem_limit_bytes=grant << 20),
        out_shape=outs,
        in_specs=in_specs,
        out_specs=[VMEM] * len(outs),
        cost_estimate=pl.CostEstimate(flops=flops, bytes_accessed=nbytes, transcendentals=0),
    )


def select_kernel(off_ref, q_ref, k_ref, v_ref, q1_ref, near_ref, kv2_ref, f3_ref, f4_ref):
    row = iota((SEL, TOK), 0)
    tok = iota((SEL, TOK), 1)
    base = jnp.where(row < 64, row * 4, jnp.where(row < 80, (row - 64) * 16, (row - 80) * 64))
    base = jnp.where(row < 84, base, 0)
    for pair in range(PAIRS):
        picks = []
        for side in range(2):
            head = 2 * pair + side
            off = jnp.where(
                row < 64,
                off_ref[1, head],
                jnp.where(row < 80, off_ref[2, head], jnp.where(row < 84, off_ref[3, head], off_ref[4, head])),
            )
            hit = (tok == base + off) & (row < 85)
            picks.append(jnp.where(hit, 1.0, 0.0).astype(BF16))
        pick = jnp.concatenate(picks, 0)
        at = lanes_of(pair)
        after = slice(WIDTH + pair * LANES, WIDTH + (pair + 1) * LANES)
        rows = join_heads(dot_nn(pick, q_ref[:, at]) * SCALE).astype(BF16)
        q1_ref[:, at] = rows[0:64]
        near_ref[64:80, at] = rows[64:80]
        near_ref[64:80, after] = rows[80:96]
        for ref, here in ((k_ref, at), (v_ref, after)):
            rows = join_heads(dot_nn(pick, ref[:, at])).astype(BF16)
            near_ref[0:64, here] = rows[0:64]
            kv2_ref[:, here] = rows[64:80]
            f3_ref[:, here] = rows[80:84]
            f4_ref[:, here] = rows[84:85]


def local_kernel(q_ref, k_ref, v_ref, acc_ref, stat_ref):
    half = TOK // 2
    for part in range(2):
        keys = (part + 1) * half
        here = slice(part * half, keys)
        query = iota((2 * half, keys), 0) % half + part * half
        allowed = iota((2 * half, keys), 1) <= query
        stats = jnp.zeros((half, LANES), F32)
        for pair in range(PAIRS):
            at = lanes_of(pair)
            queries = split_heads(q_ref[here, at] * jnp.asarray(SCALE, BF16))
            scores = jnp.where(allowed, dot_nt(queries, k_ref[0:keys, at]), NEG)
            peak = jnp.max(scores, axis=1, keepdims=True)
            weights = jnp.exp(scores - peak)
            total = jnp.sum(weights, axis=1, keepdims=True)
            acc_ref[here, at] = join_heads(dot_nn(weights.astype(BF16), v_ref[0:keys, at]))
            stats = put_stats(stats, pair, peak, total)
        stat_ref[here, :] = stats


def far_kernel(pos_ref, qa_ref, qb_ref, ka_ref, kb_ref, out_ref):
    me = pos_ref[0]
    col = iota((1, 256), 1) & 127
    block = col >> 4
    asker = me ^ ((block & 1) * 2) ^ (((block >> 1) & 1) * 6) ^ (block >> 2)
    q_row = col & 15
    row = iota((32, 1), 0)
    owner = me ^ ((row >> 4) * 8)
    allowed2 = (owner & 15) * 16 + (row & 15) <= (asker & 15) * 16 + q_row
    row = iota((64, 1), 0)
    k_row = row & 7
    owner = me ^ (((row >> 3) & 1) * 32) ^ (((row >> 4) & 1) * 16) ^ ((row >> 5) * 8)
    far_owner = owner ^ ((k_row & 1) * 192) ^ (((k_row >> 1) & 1) * 64)
    q_limit = jnp.where(q_row < 4, (asker & 63) * 4 + q_row, -1)
    third = (owner & 63) * 4 + k_row <= q_limit
    fourth = far_owner <= jnp.where(q_row == 4, asker, -1)
    allowed34 = jnp.where(k_row < 4, third.astype(jnp.int32), fourth.astype(jnp.int32)) > 0
    stat_row = iota((32, 128), 0)
    results = []
    for level, first, allowed in ((0, 0, allowed2), (1, WIDTH, allowed34)):
        low, high = ((32, 48), (0, 32))[level]
        stats = jnp.zeros((32, 128), F32)
        accs = []
        for pair in range(PAIRS):
            at = lanes_of(pair)
            vat = slice(WIDTH + pair * LANES, WIDTH + (pair + 1) * LANES)
            qat = slice(first + pair * LANES, first + (pair + 1) * LANES)
            queries = split_heads(jnp.concatenate([qa_ref[128:192, qat], qb_ref[128:192, qat]], 0))
            keys = jnp.concatenate([ka_ref[low:high, at], kb_ref[low:high, at]], 0)
            values = jnp.concatenate([ka_ref[low:high, vat], kb_ref[low:high, vat]], 0)
            scores = jnp.where(allowed, dot_nt(keys, queries), NEG)
            peak = jnp.max(scores, axis=0, keepdims=True)
            weights = jnp.where(allowed, jnp.exp(scores - peak), 0.0)
            total = jnp.sum(weights, axis=0, keepdims=True)
            acc = lax.dot_general(
                weights.astype(BF16), values, (((0,), (0,)), ((), ())), preferred_element_type=F32
            )
            accs.append(join_heads(acc).astype(BF16))
            for side in range(2):
                here = slice(128 * side, 128 * side + 128)
                stats = jnp.where(stat_row == 2 * pair + side, peak[:, here], stats)
                stats = jnp.where(stat_row == STAT + 2 * pair + side, total[:, here], stats)
        high = stats.astype(BF16).astype(F32)
        mid = (stats - high).astype(BF16).astype(F32)
        low = stats - high - mid
        stats = jnp.concatenate([high, mid, low, jnp.zeros((32, 128), F32)], 0).T.astype(BF16)
        results.append((accs, stats))
    for number in range(8):
        to = (me & 7) ^ ((number & 1) * 2) ^ (((number >> 1) & 1) * 6) ^ (number >> 2)
        for level, begin, rows in ((0, 0, 16), (1, 16, 8)):
            accs, stats = results[level]
            here = slice(number * 16, number * 16 + rows)
            for pair in range(PAIRS):
                out_ref[to, begin:begin + rows, lanes_of(pair)] = accs[pair][here]
            out_ref[to, begin:begin + rows, WIDTH:WIDTH + LANES] = stats[here]


def head_row(off_ref, level, shape, per_lane):
    lane = iota(shape, 1)
    lane = lane if per_lane else lane // HALF
    off = jnp.zeros(shape, jnp.int32)
    for head in range(HEADS):
        off = jnp.where(lane == head, off_ref[level, head], off)
    return off


def near_kernel(off_ref, pos_ref, q1_ref, a1_ref, b1_ref, acc0_ref, stat0_ref, acc_ref, stat_ref):
    me = pos_ref[0]
    col = iota((1, TOK), 1)
    device = me ^ (((col >> 6) & 1) * 2) ^ (col >> 7)
    k_pos = (device & 3) * 64 + (col & 63)
    q_pos = (me & 3) * 64 + (iota((128, 1), 0) & 63)
    allowed = k_pos <= q_pos
    stats = jnp.zeros((64, LANES), F32)
    accs = []
    for pair in range(PAIRS):
        at = lanes_of(pair)
        vat = slice(WIDTH + pair * LANES, WIDTH + (pair + 1) * LANES)
        queries = split_heads(q1_ref[:, at])
        scores = jnp.concatenate([dot_nt(queries, a1_ref[0:128, at]), dot_nt(queries, b1_ref[0:128, at])], 1)
        scores = jnp.where(allowed, scores, NEG)
        peak = jnp.max(scores, axis=1, keepdims=True)
        weights = jnp.exp(scores - peak)
        total = jnp.sum(weights, axis=1, keepdims=True)
        weights = weights.astype(BF16)
        acc = dot_nn(weights[:, 0:128], a1_ref[0:128, vat]) + dot_nn(weights[:, 128:256], b1_ref[0:128, vat])
        accs.append(join_heads(acc))
        stats = put_stats(stats, pair, peak, total)
    lane = iota((TOK, LANES), 1)
    tok = iota((TOK, LANES), 0)
    expand = jnp.where((iota((TOK, 64), 0) >> 2) == iota((TOK, 64), 1), 1.0, 0.0)
    spread = jnp.dot(expand, stats, precision=lax.Precision.HIGHEST, preferred_element_type=F32)
    kept = ((tok & 3) == head_row(off_ref, 1, (1, LANES), True)) & (lane < HEADS)
    stat0 = stat0_ref[...]
    peak0 = jnp.where(lane < HEADS, stat0, 0.0)
    peak1 = jnp.where(kept, spread, NEG)
    best = jnp.maximum(peak0, peak1)
    share0 = jnp.where(lane < HEADS, jnp.exp(peak0 - best), 0.0)
    share1 = jnp.exp(peak1 - best)
    total = share0 * pltpu.roll(stat0, LANES - STAT, 1) + share1 * pltpu.roll(spread, LANES - STAT, 1)
    stat_ref[...] = jnp.where(lane < HEADS, best, pltpu.roll(jnp.where(lane < HEADS, total, 0.0), STAT, 1))
    row_share = lax.dot_general(
        expand, share1, (((0,), (0,)), ((), ())), precision=lax.Precision.HIGHEST, preferred_element_type=F32
    )
    scale0 = over_lanes(share0)
    scale1 = over_lanes(row_share)
    twice = jnp.concatenate([expand.astype(BF16)] * 2, 1)
    for pair in range(PAIRS):
        at = lanes_of(pair)
        high, low = split2(accs[pair] * scale1[:, at])
        rows = dot_nn(twice, jnp.concatenate([high, low], 0))
        lane = iota((1, LANES), 1) >> 6
        off = jnp.where(lane == 0, off_ref[1, 2 * pair], off_ref[1, 2 * pair + 1])
        rows = jnp.where((iota((TOK, LANES), 0) & 3) == off, rows, 0.0)
        acc_ref[:, at] = scale0[:, at] * acc0_ref[:, at] + rows


def split2(value):
    high = value.astype(BF16)
    return high, (value - high.astype(F32)).astype(BF16)


def over_lanes(coeff):
    high, low = split2(coeff)
    lane = iota((2 * LANES, WIDTH), 1) // HALF
    spread = jnp.where((iota((2 * LANES, WIDTH), 0) & (LANES - 1)) == lane, 1.0, 0.0).astype(BF16)
    return dot_nn(jnp.concatenate([high, low], 1), spread)


def final_kernel(off_ref, acc_ref, stat_ref, ret_ref, out_ref):
    lane = iota((24, LANES), 1)
    parts = []
    for number in range(8):
        stats = ret_ref[number, :, WIDTH:WIDTH + LANES].astype(F32)
        parts.append(stats + pltpu.roll(stats, 96, 1) + pltpu.roll(stats, 64, 1))
    peaks = [jnp.where(lane < HEADS, part, NEG) for part in parts]
    peak = functools.reduce(jnp.maximum, peaks)
    factors = [jnp.where(lane < HEADS, jnp.exp(part - peak), 0.0) for part in peaks]
    total = sum(factor * pltpu.roll(part, LANES - STAT, 1) for factor, part in zip(factors, parts))
    spread = over_lanes(jnp.concatenate(factors, 0))
    rows = sum(
        spread[24 * number:24 * number + 24] * ret_ref[number, :, 0:WIDTH].astype(F32) for number in range(8)
    )

    def expanded(value, level):
        if level == 2:
            return jnp.concatenate([jnp.broadcast_to(value[r:r + 1], (16, LANES)) for r in range(16)], 0)
        if level == 3:
            return jnp.concatenate([jnp.broadcast_to(value[16 + r:17 + r], (64, LANES)) for r in range(4)], 0)
        return jnp.broadcast_to(value[20:21], (TOK, LANES))

    lane = iota((TOK, LANES), 1)
    tok = iota((TOK, LANES), 0)
    stat = stat_ref[...]
    level_peaks = [jnp.where(lane < HEADS, stat, 0.0)]
    level_totals = [pltpu.roll(stat, LANES - STAT, 1)]
    for level in (2, 3, 4):
        kept = ((tok & (4**level - 1)) == head_row(off_ref, level, (1, LANES), True)) & (lane < HEADS)
        level_peaks.append(jnp.where(kept, expanded(peak, level), NEG))
        level_totals.append(expanded(total, level))
    best = functools.reduce(jnp.maximum, level_peaks)
    shares = [jnp.where(lane < HEADS, jnp.exp(value - best), 0.0) for value in level_peaks]
    denom = sum(share * value for share, value in zip(shares, level_totals))
    inverse = 1.0 / jnp.where(lane < HEADS, denom, 1.0)
    shares = [share * inverse for share in shares]
    row_shares = [jnp.sum(shares[1][16 * r:16 * r + 16], axis=0, keepdims=True) for r in range(16)]
    row_shares += [jnp.sum(shares[2][64 * r:64 * r + 64], axis=0, keepdims=True) for r in range(4)]
    row_shares += [jnp.sum(shares[3], axis=0, keepdims=True)]
    row_shares += [jnp.zeros((3, LANES), F32)]
    rows = rows * over_lanes(jnp.concatenate(row_shares, 0))
    scale = over_lanes(shares[0])
    hits = [
        iota((4**level, WIDTH), 0) == head_row(off_ref, level, (1, WIDTH), False) for level in (2, 3, 4)
    ]
    for r in range(16):
        here = slice(16 * r, 16 * r + 16)
        inner = slice(16 * (r % 4), 16 * (r % 4) + 16)
        merged = scale[here] * acc_ref[here, :]
        merged = merged + jnp.where(hits[0], rows[r:r + 1], 0.0)
        merged = merged + jnp.where(hits[1][inner], rows[16 + r // 4:17 + r // 4], 0.0)
        merged = merged + jnp.where(hits[2][here], rows[20:21], 0.0)
        out_ref[here, :] = merged.astype(BF16)


def shaped(rows, width, dtype):
    return jax.ShapeDtypeStruct((rows, width), dtype)


def traded(value, mask, count):
    return lax.ppermute(value, "ctx", [(source, source ^ mask) for source in range(count)])


def grown(value, mask, count):
    return jnp.concatenate([value, traded(value, mask, count)], 0)


def program(queries, keys, values, offsets):
    count = lax.axis_size("ctx")
    me = lax.axis_index("ctx").astype(jnp.int32).reshape(1)
    q1, near, kv2, third, fourth = call(
        select_kernel,
        [shaped(64, WIDTH, BF16), shaped(80, 2 * WIDTH, BF16), shaped(16, 2 * WIDTH, BF16),
         shaped(4, 2 * WIDTH, BF16), shaped(1, 2 * WIDTH, BF16)],
        [SMEM] + [VMEM] * 3, 200_000_000, 2_000_000, 12,
    )(offsets, queries, keys, values)
    fourth = grown(fourth, 192, count)
    fourth = grown(fourth, 64, count)
    far = jnp.concatenate([third, fourth], 0)
    far = grown(far, 32, count)
    far = grown(far, 16, count)
    far = jnp.concatenate([far, kv2], 0)
    far_other = traded(far, 8, count)
    near_other = traded(near, 2, count)
    asked = jnp.concatenate([near[64:80], near_other[64:80]], 0)
    asked_other = traded(asked, 6, count)
    both = jnp.concatenate([near[0:64], near_other[0:64], asked, asked_other], 0)
    both_other = traded(both, 1, count)
    acc0, stat0 = call(
        local_kernel, [shaped(TOK, WIDTH, F32), shaped(TOK, LANES, F32)], [VMEM] * 3, 1_000_000_000, 3_000_000, 12,
    )(queries, keys, values)
    (partial,) = call(
        far_kernel, [jax.ShapeDtypeStruct((8, 24, WIDTH + LANES), BF16)], [SMEM] + [VMEM] * 4,
        200_000_000, 600_000, 12,
    )(me, both, both_other, far, far_other)
    groups = [list(range(first, first + 8)) for first in range(0, count, 8)]
    back = lax.all_to_all(partial, "ctx", 0, 0, axis_index_groups=groups)
    acc01, stat01 = call(
        near_kernel, [shaped(TOK, WIDTH, F32), shaped(TOK, LANES, F32)],
        [SMEM, SMEM] + [VMEM] * 5, 600_000_000, 2_000_000, 16,
    )(offsets, me, q1, both, both_other, acc0, stat0)
    (merged,) = call(
        final_kernel, [shaped(TOK, WIDTH, BF16)], [SMEM, VMEM, VMEM, VMEM], 1_000_000_000, 3_000_000, 16,
    )(offsets, acc01, stat01, back)
    return merged


def solution(mesh):
    in_specs = (P("ctx", None), P("ctx", None), P("ctx", None), P())
    return jax.shard_map(program, mesh=mesh, in_specs=in_specs, out_specs=P("ctx", None), check_vma=False)
```

```python
import functools

import jax
import jax.numpy as jnp
from jax import lax
from jax.experimental import pallas as pl
from jax.experimental.pallas import tpu as pltpu
from jax.sharding import PartitionSpec as P

HEADS = 12
PAIRS = 6
LANES = 128
HALF = 64
TOK = 256
WIDTH = 768
NEG = -1e30
SCALE = 0.125
F32 = jnp.float32
BF16 = jnp.bfloat16
SEL = 96
STAT = 16
VMEM = pl.BlockSpec(memory_space=pltpu.VMEM)
SMEM = pl.BlockSpec(memory_space=pltpu.SMEM)


def iota(shape, dim):
    return lax.broadcasted_iota(jnp.int32, shape, dim)


def dot_nt(a, b):
    return lax.dot_general(a, b, (((1,), (1,)), ((), ())), preferred_element_type=F32)


def dot_nn(a, b):
    return jnp.dot(a, b, preferred_element_type=F32)


def lanes_of(pair):
    return slice(pair * LANES, (pair + 1) * LANES)


def split_heads(rows):
    low = iota(rows.shape, 1) < HALF
    zero = jnp.zeros_like(rows)
    return jnp.concatenate([jnp.where(low, rows, zero), jnp.where(low, zero, rows)], 0)


def join_heads(stacked):
    n = stacked.shape[0] // 2
    low = iota((n, LANES), 1) < HALF
    return jnp.where(low, stacked[:n], stacked[n:])


def put_stats(stats, pair, peak, total):
    n = stats.shape[0]
    lane = iota(stats.shape, 1)
    for side in range(2):
        head = 2 * pair + side
        stats = jnp.where(lane == head, peak[side * n:(side + 1) * n], stats)
        stats = jnp.where(lane == STAT + head, total[side * n:(side + 1) * n], stats)
    return stats


def call(body, outs, in_specs, flops, nbytes, grant, scratch=()):
    return pl.pallas_call(
        body,
        scratch_shapes=scratch,
        compiler_params=pltpu.CompilerParams(vmem_limit_bytes=grant << 20),
        out_shape=outs,
        in_specs=in_specs,
        out_specs=[VMEM] * len(outs),
        cost_estimate=pl.CostEstimate(flops=flops, bytes_accessed=nbytes, transcendentals=0),
    )


def select_kernel(
    off_hbm, q_hbm, k_hbm, v_hbm, q1_ref, near_ref, kv2_ref, f3_ref, f4_ref, off_ref, q_ref, k_ref, v_ref, sems
):
    pairs = ((off_hbm, off_ref), (q_hbm, q_ref), (k_hbm, k_ref), (v_hbm, v_ref))
    copies = [pltpu.make_async_copy(src, dst, sems.at[n]) for n, (src, dst) in enumerate(pairs)]
    for copy in copies:
        copy.start()
    for copy in copies:
        copy.wait()
    row = iota((SEL, TOK), 0)
    tok = iota((SEL, TOK), 1)
    base = jnp.where(row < 64, row * 4, jnp.where(row < 80, (row - 64) * 16, (row - 80) * 64))
    base = jnp.where(row < 84, base, 0)
    for pair in range(PAIRS):
        picks = []
        for side in range(2):
            head = 2 * pair + side
            off = jnp.where(
                row < 64,
                off_ref[1, head],
                jnp.where(row < 80, off_ref[2, head], jnp.where(row < 84, off_ref[3, head], off_ref[4, head])),
            )
            hit = (tok == base + off) & (row < 85)
            picks.append(jnp.where(hit, 1.0, 0.0).astype(BF16))
        pick = jnp.concatenate(picks, 0)
        at = lanes_of(pair)
        after = slice(WIDTH + pair * LANES, WIDTH + (pair + 1) * LANES)
        rows = join_heads(dot_nn(pick, q_ref[:, at]) * SCALE).astype(BF16)
        q1_ref[:, at] = rows[0:64]
        near_ref[64:80, at] = rows[64:80]
        near_ref[64:80, after] = rows[80:96]
        for ref, here in ((k_ref, at), (v_ref, after)):
            rows = join_heads(dot_nn(pick, ref[:, at])).astype(BF16)
            near_ref[0:64, here] = rows[0:64]
            kv2_ref[:, here] = rows[64:80]
            f3_ref[:, here] = rows[80:84]
            f4_ref[:, here] = rows[84:85]


def local_kernel(q_ref, k_ref, v_ref, acc_ref, stat_ref):
    half = TOK // 2
    for part in range(2):
        keys = (part + 1) * half
        here = slice(part * half, keys)
        query = iota((2 * half, keys), 0) % half + part * half
        allowed = iota((2 * half, keys), 1) <= query
        stats = jnp.zeros((half, LANES), F32)
        for pair in range(PAIRS):
            at = lanes_of(pair)
            queries = split_heads(q_ref[here, at] * jnp.asarray(SCALE, BF16))
            scores = jnp.where(allowed, dot_nt(queries, k_ref[0:keys, at]), NEG)
            peak = jnp.max(scores, axis=1, keepdims=True)
            weights = jnp.exp(scores - peak)
            total = jnp.sum(weights, axis=1, keepdims=True)
            acc_ref[here, at] = join_heads(dot_nn(weights.astype(BF16), v_ref[0:keys, at]))
            stats = put_stats(stats, pair, peak, total)
        stat_ref[here, :] = stats


def far_kernel(pos_ref, qa_ref, qb_ref, ka_ref, kb_ref, kf_ref, out_ref):
    me = pos_ref[0]

    def device_of(block):
        return me ^ ((block & 1) * 2) ^ (((block >> 1) & 1) * 6) ^ (block >> 2)

    col = iota((1, 256), 1) & 127
    asker = device_of(col >> 4)
    row = iota((32, 1), 0)
    owner = me ^ ((row >> 4) * 8)
    allowed2 = (owner & 15) * 16 + (row & 15) <= (asker & 15) * 16 + (col & 15)
    col = iota((1, 128), 1) & 63
    asker = device_of(col >> 3)
    q_row = col & 7
    row = iota((64, 1), 0)
    k_row = row & 7
    owner = (me - (me & 56)) + (row >> 3) * 8
    far_owner = owner ^ ((k_row & 1) * 192) ^ (((k_row >> 1) & 1) * 64)
    third = (owner & 63) * 4 + k_row <= jnp.where(q_row < 4, (asker & 63) * 4 + q_row, -1)
    fourth = far_owner <= jnp.where(q_row == 4, asker, -1)
    allowed34 = jnp.where(k_row < 4, third.astype(jnp.int32), fourth.astype(jnp.int32)) > 0
    results = []
    for level, rows, allowed in ((0, 16, allowed2), (1, 8, allowed34)):
        count = 8 * rows
        stat_row = iota((32, count), 0)
        stats = jnp.zeros((32, count), F32)
        accs = []
        for pair in range(PAIRS):
            at = lanes_of(pair)
            vat = slice(WIDTH + pair * LANES, WIDTH + (pair + 1) * LANES)
            if level == 0:
                queries = jnp.concatenate([qa_ref[128:192, at], qb_ref[128:192, at]], 0)
                keys = jnp.concatenate([ka_ref[:, at], kb_ref[:, at]], 0)
                values = jnp.concatenate([ka_ref[:, vat], kb_ref[:, vat]], 0)
            else:
                blocks = [ref[128 + 16 * n:136 + 16 * n, vat] for ref in (qa_ref, qb_ref) for n in range(4)]
                queries = jnp.concatenate(blocks, 0)
                keys = kf_ref[:, at]
                values = kf_ref[:, vat]
            scores = jnp.where(allowed, dot_nt(keys, split_heads(queries)), NEG)
            peak = jnp.max(scores, axis=0, keepdims=True)
            weights = jnp.where(allowed, jnp.exp(scores - peak), 0.0)
            total = jnp.sum(weights, axis=0, keepdims=True)
            acc = lax.dot_general(
                weights.astype(BF16), values, (((0,), (0,)), ((), ())), preferred_element_type=F32
            )
            accs.append(join_heads(acc).astype(BF16))
            for side in range(2):
                here = slice(count * side, count * side + count)
                stats = jnp.where(stat_row == 2 * pair + side, peak[:, here], stats)
                stats = jnp.where(stat_row == STAT + 2 * pair + side, total[:, here], stats)
        high = stats.astype(BF16).astype(F32)
        mid = (stats - high).astype(BF16).astype(F32)
        low = stats - high - mid
        stats = jnp.concatenate([high, mid, low, jnp.zeros((32, count), F32)], 0).T.astype(BF16)
        results.append((accs, stats))
    for number in range(8):
        to = device_of(number) & 7
        for level, begin, rows in ((0, 0, 16), (1, 16, 8)):
            accs, stats = results[level]
            here = slice(number * rows, number * rows + rows)
            for pair in range(PAIRS):
                out_ref[to, begin:begin + rows, lanes_of(pair)] = accs[pair][here]
            out_ref[to, begin:begin + rows, WIDTH:WIDTH + LANES] = stats[here]


def head_row(off_ref, level, shape, per_lane):
    lane = iota(shape, 1)
    lane = lane if per_lane else lane // HALF
    off = jnp.zeros(shape, jnp.int32)
    for head in range(HEADS):
        off = jnp.where(lane == head, off_ref[level, head], off)
    return off


def near_kernel(off_ref, pos_ref, q1_ref, a1_ref, b1_ref, acc0_ref, stat0_ref, acc_ref, stat_ref):
    me = pos_ref[0]
    col = iota((1, TOK), 1)
    device = me ^ (((col >> 6) & 1) * 2) ^ (col >> 7)
    k_pos = (device & 3) * 64 + (col & 63)
    q_pos = (me & 3) * 64 + (iota((128, 1), 0) & 63)
    allowed = k_pos <= q_pos
    stats = jnp.zeros((64, LANES), F32)
    accs = []
    for pair in range(PAIRS):
        at = lanes_of(pair)
        vat = slice(WIDTH + pair * LANES, WIDTH + (pair + 1) * LANES)
        queries = split_heads(q1_ref[:, at])
        scores = jnp.concatenate([dot_nt(queries, a1_ref[0:128, at]), dot_nt(queries, b1_ref[0:128, at])], 1)
        scores = jnp.where(allowed, scores, NEG)
        peak = jnp.max(scores, axis=1, keepdims=True)
        weights = jnp.exp(scores - peak)
        total = jnp.sum(weights, axis=1, keepdims=True)
        weights = weights.astype(BF16)
        acc = dot_nn(weights[:, 0:128], a1_ref[0:128, vat]) + dot_nn(weights[:, 128:256], b1_ref[0:128, vat])
        accs.append(join_heads(acc))
        stats = put_stats(stats, pair, peak, total)
    lane = iota((TOK, LANES), 1)
    tok = iota((TOK, LANES), 0)
    expand = jnp.where((iota((TOK, 64), 0) >> 2) == iota((TOK, 64), 1), 1.0, 0.0)
    spread = jnp.dot(expand, stats, precision=lax.Precision.HIGHEST, preferred_element_type=F32)
    kept = ((tok & 3) == head_row(off_ref, 1, (1, LANES), True)) & (lane < HEADS)
    stat0 = stat0_ref[...]
    peak0 = jnp.where(lane < HEADS, stat0, 0.0)
    peak1 = jnp.where(kept, spread, NEG)
    best = jnp.maximum(peak0, peak1)
    share0 = jnp.where(lane < HEADS, jnp.exp(peak0 - best), 0.0)
    share1 = jnp.exp(peak1 - best)
    total = share0 * pltpu.roll(stat0, LANES - STAT, 1) + share1 * pltpu.roll(spread, LANES - STAT, 1)
    stat_ref[...] = jnp.where(lane < HEADS, best, pltpu.roll(jnp.where(lane < HEADS, total, 0.0), STAT, 1))
    row_share = lax.dot_general(
        expand, share1, (((0,), (0,)), ((), ())), precision=lax.Precision.HIGHEST, preferred_element_type=F32
    )
    scale0 = over_lanes(share0)
    scale1 = over_lanes(row_share)
    twice = jnp.concatenate([expand.astype(BF16)] * 2, 1)
    for pair in range(PAIRS):
        at = lanes_of(pair)
        high, low = split2(accs[pair] * scale1[:, at])
        rows = dot_nn(twice, jnp.concatenate([high, low], 0))
        lane = iota((1, LANES), 1) >> 6
        off = jnp.where(lane == 0, off_ref[1, 2 * pair], off_ref[1, 2 * pair + 1])
        rows = jnp.where((iota((TOK, LANES), 0) & 3) == off, rows, 0.0)
        acc_ref[:, at] = scale0[:, at] * acc0_ref[:, at] + rows


def split2(value):
    high = value.astype(BF16)
    return high, (value - high.astype(F32)).astype(BF16)


def over_lanes(coeff):
    high, low = split2(coeff)
    lane = iota((2 * LANES, WIDTH), 1) // HALF
    spread = jnp.where((iota((2 * LANES, WIDTH), 0) & (LANES - 1)) == lane, 1.0, 0.0).astype(BF16)
    return dot_nn(jnp.concatenate([high, low], 1), spread)


def final_kernel(off_ref, acc_ref, stat_ref, ret_ref, out_ref):
    lane = iota((24, LANES), 1)
    parts = []
    for number in range(8):
        stats = ret_ref[number, :, WIDTH:WIDTH + LANES].astype(F32)
        parts.append(stats + pltpu.roll(stats, 96, 1) + pltpu.roll(stats, 64, 1))
    peaks = [jnp.where(lane < HEADS, part, NEG) for part in parts]
    peak = functools.reduce(jnp.maximum, peaks)
    factors = [jnp.where(lane < HEADS, jnp.exp(part - peak), 0.0) for part in peaks]
    total = sum(factor * pltpu.roll(part, LANES - STAT, 1) for factor, part in zip(factors, parts))
    spread = over_lanes(jnp.concatenate(factors, 0))
    rows = sum(
        spread[24 * number:24 * number + 24] * ret_ref[number, :, 0:WIDTH].astype(F32) for number in range(8)
    )

    def expanded(value, level):
        if level == 2:
            return jnp.concatenate([jnp.broadcast_to(value[r:r + 1], (16, LANES)) for r in range(16)], 0)
        if level == 3:
            return jnp.concatenate([jnp.broadcast_to(value[16 + r:17 + r], (64, LANES)) for r in range(4)], 0)
        return jnp.broadcast_to(value[20:21], (TOK, LANES))

    lane = iota((TOK, LANES), 1)
    tok = iota((TOK, LANES), 0)
    stat = stat_ref[...]
    level_peaks = [jnp.where(lane < HEADS, stat, 0.0)]
    level_totals = [pltpu.roll(stat, LANES - STAT, 1)]
    for level in (2, 3, 4):
        kept = ((tok & (4**level - 1)) == head_row(off_ref, level, (1, LANES), True)) & (lane < HEADS)
        level_peaks.append(jnp.where(kept, expanded(peak, level), NEG))
        level_totals.append(expanded(total, level))
    best = functools.reduce(jnp.maximum, level_peaks)
    shares = [jnp.where(lane < HEADS, jnp.exp(value - best), 0.0) for value in level_peaks]
    denom = sum(share * value for share, value in zip(shares, level_totals))
    inverse = 1.0 / jnp.where(lane < HEADS, denom, 1.0)
    shares = [share * inverse for share in shares]
    row_shares = [jnp.sum(shares[1][16 * r:16 * r + 16], axis=0, keepdims=True) for r in range(16)]
    row_shares += [jnp.sum(shares[2][64 * r:64 * r + 64], axis=0, keepdims=True) for r in range(4)]
    row_shares += [jnp.sum(shares[3], axis=0, keepdims=True)]
    row_shares += [jnp.zeros((3, LANES), F32)]
    rows = rows * over_lanes(jnp.concatenate(row_shares, 0))
    scale = over_lanes(shares[0])
    hits = [
        iota((4**level, WIDTH), 0) == head_row(off_ref, level, (1, WIDTH), False) for level in (2, 3, 4)
    ]
    for r in range(16):
        here = slice(16 * r, 16 * r + 16)
        inner = slice(16 * (r % 4), 16 * (r % 4) + 16)
        merged = scale[here] * acc_ref[here, :]
        merged = merged + jnp.where(hits[0], rows[r:r + 1], 0.0)
        merged = merged + jnp.where(hits[1][inner], rows[16 + r // 4:17 + r // 4], 0.0)
        merged = merged + jnp.where(hits[2][here], rows[20:21], 0.0)
        out_ref[here, :] = merged.astype(BF16)


def shaped(rows, width, dtype):
    return jax.ShapeDtypeStruct((rows, width), dtype)


def traded(value, mask, count):
    return lax.ppermute(value, "ctx", [(source, source ^ mask) for source in range(count)])


def grown(value, mask, count):
    return jnp.concatenate([value, traded(value, mask, count)], 0)


def program(queries, keys, values, offsets):
    count = lax.axis_size("ctx")
    me = lax.axis_index("ctx").astype(jnp.int32).reshape(1)
    q1, near, kv2, third, fourth = call(
        select_kernel,
        [shaped(64, WIDTH, BF16), shaped(80, 2 * WIDTH, BF16), shaped(16, 2 * WIDTH, BF16),
         shaped(4, 2 * WIDTH, BF16), shaped(1, 2 * WIDTH, BF16)],
        [pl.BlockSpec(memory_space=pltpu.HBM)] * 4, 200_000_000, 2_000_000, 12,
        [pltpu.SMEM((5, HEADS), jnp.int32)] + [pltpu.VMEM((TOK, WIDTH), BF16)] * 3 + [pltpu.SemaphoreType.DMA((4,))],
    )(*[pltpu.with_memory_space_constraint(a, pltpu.HBM) for a in (offsets, queries, keys, values)])
    fourth = grown(fourth, 192, count)
    fourth = grown(fourth, 64, count)
    far = jnp.concatenate([third, fourth], 0)
    lines = [[first + step for step in range(0, 64, 8)] for first in range(count) if not first & 56]
    far = jnp.broadcast_to(far[None], (8, 8, 2 * WIDTH))
    far = lax.all_to_all(far, "ctx", 0, 0, axis_index_groups=lines).reshape(64, 2 * WIDTH)
    kv2_other = traded(kv2, 8, count)
    near_other = traded(near, 2, count)
    asked = jnp.concatenate([near[64:80], near_other[64:80]], 0)
    asked_other = traded(asked, 6, count)
    both = jnp.concatenate([near[0:64], near_other[0:64], asked, asked_other], 0)
    both_other = traded(both, 1, count)
    acc0, stat0 = call(
        local_kernel, [shaped(TOK, WIDTH, F32), shaped(TOK, LANES, F32)], [VMEM] * 3, 1_000_000_000, 3_000_000, 12,
    )(queries, keys, values)
    (partial,) = call(
        far_kernel, [jax.ShapeDtypeStruct((8, 24, WIDTH + LANES), BF16)], [SMEM] + [VMEM] * 5,
        200_000_000, 600_000, 12,
    )(me, both, both_other, kv2, kv2_other, far)
    groups = [list(range(first, first + 8)) for first in range(0, count, 8)]
    back = lax.all_to_all(partial, "ctx", 0, 0, axis_index_groups=groups)
    acc01, stat01 = call(
        near_kernel, [shaped(TOK, WIDTH, F32), shaped(TOK, LANES, F32)],
        [SMEM, SMEM] + [VMEM] * 5, 600_000_000, 2_000_000, 16,
    )(offsets, me, q1, both, both_other, acc0, stat0)
    (merged,) = call(
        final_kernel, [shaped(TOK, WIDTH, BF16)], [SMEM, VMEM, VMEM, VMEM], 1_000_000_000, 3_000_000, 16,
    )(offsets, acc01, stat01, back)
    return merged


def solution(mesh):
    in_specs = (P("ctx", None), P("ctx", None), P("ctx", None), P())
    return jax.shard_map(program, mesh=mesh, in_specs=in_specs, out_specs=P("ctx", None), check_vma=False)
```

```python
import functools

import jax
import jax.numpy as jnp
from jax import lax
from jax.experimental import pallas as pl
from jax.experimental.pallas import tpu as pltpu
from jax.sharding import PartitionSpec as P

HEADS = 12
PAIRS = 6
LANES = 128
HALF = 64
TOK = 256
WIDTH = 768
NEG = -1e30
SCALE = 0.125
F32 = jnp.float32
BF16 = jnp.bfloat16
SEL = 96
STAT = 16
VMEM = pl.BlockSpec(memory_space=pltpu.VMEM)
SMEM = pl.BlockSpec(memory_space=pltpu.SMEM)


def iota(shape, dim):
    return lax.broadcasted_iota(jnp.int32, shape, dim)


def dot_nt(a, b):
    return lax.dot_general(a, b, (((1,), (1,)), ((), ())), preferred_element_type=F32)


def dot_nn(a, b):
    return jnp.dot(a, b, preferred_element_type=F32)


def lanes_of(pair):
    return slice(pair * LANES, (pair + 1) * LANES)


def split_heads(rows):
    low = iota(rows.shape, 1) < HALF
    zero = jnp.zeros_like(rows)
    return jnp.concatenate([jnp.where(low, rows, zero), jnp.where(low, zero, rows)], 0)


def join_heads(stacked):
    n = stacked.shape[0] // 2
    low = iota((n, LANES), 1) < HALF
    return jnp.where(low, stacked[:n], stacked[n:])


def put_stats(stats, pair, peak, total):
    n = stats.shape[0]
    lane = iota(stats.shape, 1)
    for side in range(2):
        head = 2 * pair + side
        stats = jnp.where(lane == head, peak[side * n:(side + 1) * n], stats)
        stats = jnp.where(lane == STAT + head, total[side * n:(side + 1) * n], stats)
    return stats


def call(body, outs, in_specs, flops, nbytes, grant, scratch=()):
    return pl.pallas_call(
        body,
        scratch_shapes=scratch,
        compiler_params=pltpu.CompilerParams(vmem_limit_bytes=grant << 20),
        out_shape=outs,
        in_specs=in_specs,
        out_specs=[VMEM] * len(outs),
        cost_estimate=pl.CostEstimate(flops=flops, bytes_accessed=nbytes, transcendentals=0),
    )


def select_kernel(
    off_hbm, q_hbm, k_hbm, v_hbm, q_ref, k_ref, v_ref, q1_ref, q2_ref, kv1_ref, early_ref, f3_ref, f4_ref, off_ref, sems
):
    pairs = ((off_hbm, off_ref), (q_hbm, q_ref), (k_hbm, k_ref), (v_hbm, v_ref))
    copies = [pltpu.make_async_copy(src, dst, sems.at[n]) for n, (src, dst) in enumerate(pairs)]
    for copy in copies:
        copy.start()
    for copy in copies:
        copy.wait()
    row = iota((SEL, TOK), 0)
    tok = iota((SEL, TOK), 1)
    base = jnp.where(row < 64, row * 4, jnp.where(row < 80, (row - 64) * 16, (row - 80) * 64))
    base = jnp.where(row < 84, base, 0)
    early_ref[16:24, WIDTH:2 * WIDTH] = jnp.zeros((8, WIDTH), BF16)
    for pair in range(PAIRS):
        picks = []
        for side in range(2):
            head = 2 * pair + side
            off = jnp.where(
                row < 64,
                off_ref[1, head],
                jnp.where(row < 80, off_ref[2, head], jnp.where(row < 84, off_ref[3, head], off_ref[4, head])),
            )
            hit = (tok == base + off) & (row < 85)
            picks.append(jnp.where(hit, 1.0, 0.0).astype(BF16))
        pick = jnp.concatenate(picks, 0)
        at = lanes_of(pair)
        after = slice(WIDTH + pair * LANES, WIDTH + (pair + 1) * LANES)
        rows = join_heads(dot_nn(pick, q_ref[:, at]) * SCALE).astype(BF16)
        q1_ref[:, at] = rows[0:64]
        q2_ref[:, at] = rows[64:80]
        early_ref[16:24, at] = rows[80:88]
        for ref, here in ((k_ref, at), (v_ref, after)):
            rows = join_heads(dot_nn(pick, ref[:, at])).astype(BF16)
            kv1_ref[:, here] = rows[0:64]
            early_ref[0:16, here] = rows[64:80]
            f3_ref[:, here] = rows[80:84]
            f4_ref[:, here] = rows[84:85]


def local_kernel(q_ref, k_ref, v_ref, acc_ref):
    half = TOK // 2
    for part in range(2):
        keys = (part + 1) * half
        here = slice(part * half, keys)
        query = iota((2 * half, keys), 0) % half + part * half
        allowed = iota((2 * half, keys), 1) <= query
        stats = jnp.zeros((half, LANES), F32)
        for pair in range(PAIRS):
            at = lanes_of(pair)
            queries = split_heads(q_ref[here, at] * jnp.asarray(SCALE, BF16))
            scores = jnp.where(allowed, dot_nt(queries, k_ref[0:keys, at]), NEG)
            peak = jnp.max(scores, axis=1, keepdims=True)
            weights = jnp.exp(scores - peak)
            total = jnp.sum(weights, axis=1, keepdims=True)
            acc_ref[here, at] = join_heads(dot_nn(weights.astype(BF16), v_ref[0:keys, at]))
            stats = put_stats(stats, pair, peak, total)
        acc_ref[here, WIDTH:WIDTH + LANES] = stats


def far_kernel(pos_ref, qa_ref, qb_ref, kf_ref, out_ref):
    me = pos_ref[0]

    def device_of(block):
        return me ^ ((block & 1) * 2) ^ (((block >> 1) & 1) * 6) ^ (block >> 2)

    col = iota((1, 128), 1) & 63
    asker = device_of(col >> 3)
    q_row = col & 7
    row = iota((64, 1), 0)
    k_row = row & 7
    owner = (me - (me & 56)) + (row >> 3) * 8
    far_owner = owner ^ ((k_row & 1) * 192) ^ (((k_row >> 1) & 1) * 64)
    third = (owner & 63) * 4 + k_row <= jnp.where(q_row < 4, (asker & 63) * 4 + q_row, -1)
    fourth = far_owner <= jnp.where(q_row == 4, asker, -1)
    allowed = jnp.where(k_row < 4, third.astype(jnp.int32), fourth.astype(jnp.int32)) > 0
    stat_row = iota((32, 64), 0)
    stats = jnp.zeros((32, 64), F32)
    accs = []
    for pair in range(PAIRS):
        at = lanes_of(pair)
        vat = slice(WIDTH + pair * LANES, WIDTH + (pair + 1) * LANES)
        queries = split_heads(jnp.concatenate([qa_ref[:, at], qb_ref[:, at]], 0))
        scores = jnp.where(allowed, dot_nt(kf_ref[:, at], queries), NEG)
        peak = jnp.max(scores, axis=0, keepdims=True)
        weights = jnp.where(allowed, jnp.exp(scores - peak), 0.0)
        total = jnp.sum(weights, axis=0, keepdims=True)
        acc = lax.dot_general(
            weights.astype(BF16), kf_ref[:, vat], (((0,), (0,)), ((), ())), preferred_element_type=F32
        )
        accs.append(join_heads(acc).astype(BF16))
        for side in range(2):
            here = slice(64 * side, 64 * side + 64)
            stats = jnp.where(stat_row == 2 * pair + side, peak[:, here], stats)
            stats = jnp.where(stat_row == STAT + 2 * pair + side, total[:, here], stats)
    high = stats.astype(BF16).astype(F32)
    mid = (stats - high).astype(BF16).astype(F32)
    low = stats - high - mid
    stats = jnp.concatenate([high, mid, low, jnp.zeros((32, 64), F32)], 0).T.astype(BF16)
    for number in range(8):
        to = device_of(number) & 7
        here = slice(number * 8, number * 8 + 8)
        for pair in range(PAIRS):
            out_ref[to, :, lanes_of(pair)] = accs[pair][here]
        out_ref[to, :, WIDTH:WIDTH + LANES] = stats[here]


def head_row(off_ref, level, shape, per_lane):
    lane = iota(shape, 1)
    lane = lane if per_lane else lane // HALF
    off = jnp.zeros(shape, jnp.int32)
    for head in range(HEADS):
        off = jnp.where(lane == head, off_ref[level, head], off)
    return off


def gathered(q_ref, parts, rows, allowed):
    stats = jnp.zeros((rows, LANES), F32)
    accs = []
    for pair in range(PAIRS):
        at = lanes_of(pair)
        vat = slice(WIDTH + pair * LANES, WIDTH + (pair + 1) * LANES)
        queries = split_heads(q_ref[:, at])
        scores = jnp.concatenate([dot_nt(queries, ref[:, at]) for ref in parts], 1)
        scores = jnp.where(allowed, scores, NEG)
        peak = jnp.max(scores, axis=1, keepdims=True)
        weights = jnp.exp(scores - peak)
        total = jnp.sum(weights, axis=1, keepdims=True)
        weights = weights.astype(BF16)
        acc = dot_nn(weights[:, 0:128], parts[0][:, vat]) + dot_nn(weights[:, 128:256], parts[1][:, vat])
        accs.append(join_heads(acc))
        stats = put_stats(stats, pair, peak, total)
    return accs, stats


def absorb(off_ref, level, accs, stats, acc_ref, out_ref):
    group = 4**level
    rows = TOK // group
    lane = iota((TOK, LANES), 1)
    tok = iota((TOK, LANES), 0)
    expand = jnp.where((iota((TOK, rows), 0) >> (2 * level)) == iota((TOK, rows), 1), 1.0, 0.0)
    spread = jnp.dot(expand, stats, precision=lax.Precision.HIGHEST, preferred_element_type=F32)
    kept = ((tok & (group - 1)) == head_row(off_ref, level, (1, LANES), True)) & (lane < HEADS)
    stat = acc_ref[:, WIDTH:WIDTH + LANES]
    peak0 = jnp.where(lane < HEADS, stat, 0.0)
    peak1 = jnp.where(kept, spread, NEG)
    best = jnp.maximum(peak0, peak1)
    share0 = jnp.where(lane < HEADS, jnp.exp(peak0 - best), 0.0)
    share1 = jnp.exp(peak1 - best)
    total = share0 * pltpu.roll(stat, LANES - STAT, 1) + share1 * pltpu.roll(spread, LANES - STAT, 1)
    out_ref[:, WIDTH:WIDTH + LANES] = jnp.where(
        lane < HEADS, best, pltpu.roll(jnp.where(lane < HEADS, total, 0.0), STAT, 1)
    )
    row_share = lax.dot_general(
        expand, share1, (((0,), (0,)), ((), ())), precision=lax.Precision.HIGHEST, preferred_element_type=F32
    )
    scale0 = over_lanes(share0)
    scale1 = over_lanes(row_share)
    twice = jnp.concatenate([expand.astype(BF16)] * 2, 1)
    for pair in range(PAIRS):
        at = lanes_of(pair)
        high, low = split2(accs[pair] * scale1[:, at])
        added = dot_nn(twice, jnp.concatenate([high, low], 0))
        side = iota((1, LANES), 1) >> 6
        off = jnp.where(side == 0, off_ref[level, 2 * pair], off_ref[level, 2 * pair + 1])
        added = jnp.where((iota((TOK, LANES), 0) & (group - 1)) == off, added, 0.0)
        out_ref[:, at] = scale0[:, at] * acc_ref[:, at] + added


def first_kernel(off_ref, pos_ref, q1_ref, a_ref, b_ref, acc_ref, out_ref):
    me = pos_ref[0]
    col = iota((1, TOK), 1)
    device = me ^ (((col >> 6) & 1) * 2) ^ (col >> 7)
    k_pos = (device & 3) * 64 + (col & 63)
    q_pos = (me & 3) * 64 + (iota((128, 1), 0) & 63)
    accs, stats = gathered(q1_ref, (a_ref, b_ref), 64, k_pos <= q_pos)
    absorb(off_ref, 1, accs, stats, acc_ref, out_ref)


def second_kernel(off_ref, pos_ref, q2_ref, a_ref, b_ref, acc_ref, out_ref):
    me = pos_ref[0]
    col = iota((1, TOK), 1)
    block = (col >> 4) & 3
    device = me ^ ((block & 1) * 2) ^ ((block >> 1) * 6) ^ (((col >> 6) & 1) * 8) ^ (col >> 7)
    k_pos = (device & 15) * 16 + (col & 15)
    q_pos = (me & 15) * 16 + (iota((32, 1), 0) & 15)
    accs, stats = gathered(q2_ref, (a_ref, b_ref), 16, k_pos <= q_pos)
    absorb(off_ref, 2, accs, stats, acc_ref, out_ref)


def split2(value):
    high = value.astype(BF16)
    return high, (value - high.astype(F32)).astype(BF16)


def over_lanes(coeff):
    high, low = split2(coeff)
    lane = iota((2 * LANES, WIDTH), 1) // HALF
    spread = jnp.where((iota((2 * LANES, WIDTH), 0) & (LANES - 1)) == lane, 1.0, 0.0).astype(BF16)
    return dot_nn(jnp.concatenate([high, low], 1), spread)


def final_kernel(off_ref, acc_ref, ret_ref, out_ref):
    lane = iota((8, LANES), 1)
    parts = []
    for number in range(8):
        stats = ret_ref[number, :, WIDTH:WIDTH + LANES].astype(F32)
        parts.append(stats + pltpu.roll(stats, 96, 1) + pltpu.roll(stats, 64, 1))
    peaks = [jnp.where(lane < HEADS, part, NEG) for part in parts]
    peak = functools.reduce(jnp.maximum, peaks)
    factors = [jnp.where(lane < HEADS, jnp.exp(part - peak), 0.0) for part in peaks]
    total = sum(factor * pltpu.roll(part, LANES - STAT, 1) for factor, part in zip(factors, parts))
    spread = over_lanes(jnp.concatenate(factors, 0))
    rows = sum(
        spread[8 * number:8 * number + 8] * ret_ref[number, :, 0:WIDTH].astype(F32) for number in range(8)
    )

    def expanded(value, level):
        if level == 3:
            return jnp.concatenate([jnp.broadcast_to(value[r:r + 1], (64, LANES)) for r in range(4)], 0)
        return jnp.broadcast_to(value[4:5], (TOK, LANES))

    lane = iota((TOK, LANES), 1)
    tok = iota((TOK, LANES), 0)
    stat = acc_ref[:, WIDTH:WIDTH + LANES]
    level_peaks = [jnp.where(lane < HEADS, stat, 0.0)]
    level_totals = [pltpu.roll(stat, LANES - STAT, 1)]
    for level in (3, 4):
        kept = ((tok & (4**level - 1)) == head_row(off_ref, level, (1, LANES), True)) & (lane < HEADS)
        level_peaks.append(jnp.where(kept, expanded(peak, level), NEG))
        level_totals.append(expanded(total, level))
    best = functools.reduce(jnp.maximum, level_peaks)
    shares = [jnp.where(lane < HEADS, jnp.exp(value - best), 0.0) for value in level_peaks]
    denom = sum(share * value for share, value in zip(shares, level_totals))
    inverse = 1.0 / jnp.where(lane < HEADS, denom, 1.0)
    shares = [share * inverse for share in shares]
    row_shares = [jnp.sum(shares[1][64 * r:64 * r + 64], axis=0, keepdims=True) for r in range(4)]
    row_shares += [jnp.sum(shares[2], axis=0, keepdims=True), jnp.zeros((3, LANES), F32)]
    rows = rows * over_lanes(jnp.concatenate(row_shares, 0))
    scale = over_lanes(shares[0])
    hits = [
        iota((4**level, WIDTH), 0) == head_row(off_ref, level, (1, WIDTH), False) for level in (3, 4)
    ]
    for r in range(16):
        here = slice(16 * r, 16 * r + 16)
        inner = slice(16 * (r % 4), 16 * (r % 4) + 16)
        merged = scale[here] * acc_ref[here, 0:WIDTH]
        merged = merged + jnp.where(hits[0][inner], rows[r // 4:r // 4 + 1], 0.0)
        merged = merged + jnp.where(hits[1][here], rows[4:5], 0.0)
        out_ref[here, :] = merged.astype(BF16)


def shaped(rows, width, dtype):
    return jax.ShapeDtypeStruct((rows, width), dtype)


def traded(value, mask, count):
    return lax.ppermute(value, "ctx", [(source, source ^ mask) for source in range(count)])


def grown(value, mask, count):
    return jnp.concatenate([value, traded(value, mask, count)], 0)


def program(queries, keys, values, offsets):
    count = lax.axis_size("ctx")
    me = lax.axis_index("ctx").astype(jnp.int32).reshape(1)
    wide = 2 * WIDTH
    inputs = [pltpu.with_memory_space_constraint(a, pltpu.HBM) for a in (offsets, queries, keys, values)]
    q, k, v, q1, q2, kv1, early, third, fourth = call(
        select_kernel,
        [shaped(TOK, WIDTH, BF16)] * 3
        + [shaped(64, WIDTH, BF16), shaped(16, WIDTH, BF16), shaped(64, wide, BF16), shaped(24, wide, BF16),
           shaped(4, wide, BF16), shaped(1, wide, BF16)],
        [pl.BlockSpec(memory_space=pltpu.HBM)] * 4, 200_000_000, 2_000_000, 12,
        [pltpu.SMEM((5, HEADS), jnp.int32), pltpu.SemaphoreType.DMA((4,))],
    )(*inputs)
    fourth = grown(fourth, 192, count)
    fourth = grown(fourth, 64, count)
    far = jnp.broadcast_to(jnp.concatenate([third, fourth], 0)[None], (8, 8, wide))
    lines = [[first + step for step in range(0, 64, 8)] for first in range(count) if not first & 56]
    far = lax.all_to_all(far, "ctx", 0, 0, axis_index_groups=lines).reshape(64, wide)
    early = grown(early, 2, count)
    early = grown(early, 6, count).reshape(4, 24, wide)
    asked = early[:, 16:24, 0:WIDTH].reshape(32, WIDTH)
    asked_other = traded(asked, 1, count)
    kv1 = grown(kv1, 2, count)
    kv1_other = traded(kv1, 1, count)
    kv2 = grown(early[:, 0:16].reshape(64, wide), 8, count)
    kv2_other = traded(kv2, 1, count)
    total = shaped(TOK, WIDTH + LANES, F32)
    (acc,) = call(local_kernel, [total], [VMEM] * 3, 1_000_000_000, 3_000_000, 12)(q, k, v)
    (acc,) = call(first_kernel, [total], [SMEM, SMEM] + [VMEM] * 4, 600_000_000, 2_000_000, 16)(
        offsets, me, q1, kv1, kv1_other, acc
    )
    (partial,) = call(
        far_kernel, [jax.ShapeDtypeStruct((8, 8, WIDTH + LANES), BF16)], [SMEM] + [VMEM] * 3,
        200_000_000, 600_000, 12,
    )(me, asked, asked_other, far)
    groups = [list(range(first, first + 8)) for first in range(0, count, 8)]
    back = lax.all_to_all(partial, "ctx", 0, 0, axis_index_groups=groups)
    (acc,) = call(second_kernel, [total], [SMEM, SMEM] + [VMEM] * 4, 600_000_000, 2_000_000, 16)(
        offsets, me, q2, kv2, kv2_other, acc
    )
    (merged,) = call(
        final_kernel, [shaped(TOK, WIDTH, BF16)], [SMEM, VMEM, VMEM], 1_000_000_000, 3_000_000, 16
    )(offsets, acc, back)
    return merged


def solution(mesh):
    in_specs = (P("ctx", None), P("ctx", None), P("ctx", None), P())
    return jax.shard_map(program, mesh=mesh, in_specs=in_specs, out_specs=P("ctx", None), check_vma=False)
```

```python
import functools

import jax
import jax.numpy as jnp
from jax import lax
from jax.experimental import pallas as pl
from jax.experimental.pallas import tpu as pltpu
from jax.sharding import PartitionSpec as P

HEADS = 12
PAIRS = 6
LANES = 128
HALF = 64
TOK = 256
WIDTH = 768
NEG = -1e30
SCALE = 0.125
F32 = jnp.float32
BF16 = jnp.bfloat16
SEL = 96
STAT = 16
VMEM = pl.BlockSpec(memory_space=pltpu.VMEM)
SMEM = pl.BlockSpec(memory_space=pltpu.SMEM)


def iota(shape, dim):
    return lax.broadcasted_iota(jnp.int32, shape, dim)


def dot_nt(a, b):
    return lax.dot_general(a, b, (((1,), (1,)), ((), ())), preferred_element_type=F32)


def dot_nn(a, b):
    return jnp.dot(a, b, preferred_element_type=F32)


def lanes_of(pair):
    return slice(pair * LANES, (pair + 1) * LANES)


def split_heads(rows):
    low = iota(rows.shape, 1) < HALF
    zero = jnp.zeros_like(rows)
    return jnp.concatenate([jnp.where(low, rows, zero), jnp.where(low, zero, rows)], 0)


def join_heads(stacked):
    n = stacked.shape[0] // 2
    low = iota((n, LANES), 1) < HALF
    return jnp.where(low, stacked[:n], stacked[n:])


def put_stats(stats, pair, peak, total):
    n = stats.shape[0]
    lane = iota(stats.shape, 1)
    for side in range(2):
        head = 2 * pair + side
        stats = jnp.where(lane == head, peak[side * n:(side + 1) * n], stats)
        stats = jnp.where(lane == STAT + head, total[side * n:(side + 1) * n], stats)
    return stats


def call(body, outs, in_specs, flops, nbytes, grant, scratch=()):
    return pl.pallas_call(
        body,
        scratch_shapes=scratch,
        compiler_params=pltpu.CompilerParams(vmem_limit_bytes=grant << 20),
        out_shape=outs,
        in_specs=in_specs,
        out_specs=[VMEM] * len(outs),
        cost_estimate=pl.CostEstimate(flops=flops, bytes_accessed=nbytes, transcendentals=0),
    )


def select_kernel(
    off_hbm, q_hbm, k_hbm, v_hbm, q_ref, k_ref, v_ref, q1_ref, q2_ref, kv1_ref, early_ref, f3_ref, f4_ref, off_ref, sems
):
    pairs = ((off_hbm, off_ref), (q_hbm, q_ref), (k_hbm, k_ref), (v_hbm, v_ref))
    copies = [pltpu.make_async_copy(src, dst, sems.at[n]) for n, (src, dst) in enumerate(pairs)]
    for copy in copies:
        copy.start()
    for copy in copies:
        copy.wait()
    row = iota((SEL, TOK), 0)
    tok = iota((SEL, TOK), 1)
    base = jnp.where(row < 64, row * 4, jnp.where(row < 80, (row - 64) * 16, (row - 80) * 64))
    base = jnp.where(row < 84, base, 0)
    early_ref[16:24, WIDTH:2 * WIDTH] = jnp.zeros((8, WIDTH), BF16)
    for pair in range(PAIRS):
        picks = []
        for side in range(2):
            head = 2 * pair + side
            off = jnp.where(
                row < 64,
                off_ref[1, head],
                jnp.where(row < 80, off_ref[2, head], jnp.where(row < 84, off_ref[3, head], off_ref[4, head])),
            )
            hit = (tok == base + off) & (row < 85)
            picks.append(jnp.where(hit, 1.0, 0.0).astype(BF16))
        pick = jnp.concatenate(picks, 0)
        at = lanes_of(pair)
        after = slice(WIDTH + pair * LANES, WIDTH + (pair + 1) * LANES)
        rows = join_heads(dot_nn(pick, q_ref[:, at]) * SCALE).astype(BF16)
        q1_ref[:, at] = rows[0:64]
        q2_ref[:, at] = rows[64:80]
        early_ref[16:24, at] = rows[80:88]
        for ref, here in ((k_ref, at), (v_ref, after)):
            rows = join_heads(dot_nn(pick, ref[:, at])).astype(BF16)
            kv1_ref[:, here] = rows[0:64]
            early_ref[0:16, here] = rows[64:80]
            f3_ref[:, here] = rows[80:84]
            f4_ref[:, here] = rows[84:85]


def local_kernel(q_ref, k_ref, v_ref, acc_ref):
    half = TOK // 2
    for part in range(2):
        keys = (part + 1) * half
        here = slice(part * half, keys)
        query = iota((2 * half, keys), 0) % half + part * half
        allowed = iota((2 * half, keys), 1) <= query
        stats = jnp.zeros((half, LANES), F32)
        for pair in range(PAIRS):
            at = lanes_of(pair)
            queries = split_heads(q_ref[here, at] * jnp.asarray(SCALE, BF16))
            scores = jnp.where(allowed, dot_nt(queries, k_ref[0:keys, at]), NEG)
            peak = jnp.max(scores, axis=1, keepdims=True)
            weights = jnp.exp(scores - peak)
            total = jnp.sum(weights, axis=1, keepdims=True)
            acc_ref[here, at] = join_heads(dot_nn(weights.astype(BF16), v_ref[0:keys, at]))
            stats = put_stats(stats, pair, peak, total)
        acc_ref[here, WIDTH:WIDTH + LANES] = stats


def far_kernel(pos_ref, qa_ref, qb_ref, kf_ref, out_ref):
    me = pos_ref[0]

    def device_of(block):
        return me ^ ((block & 1) * 2) ^ (((block >> 1) & 1) * 6) ^ (block >> 2)

    col = iota((1, 128), 1) & 63
    asker = device_of(col >> 3)
    q_row = col & 7
    row = iota((64, 1), 0)
    k_row = row & 7
    owner = (me - (me & 56)) + (row >> 3) * 8
    far_owner = owner ^ ((k_row & 1) * 192) ^ (((k_row >> 1) & 1) * 64)
    third = (owner & 63) * 4 + k_row <= jnp.where(q_row < 4, (asker & 63) * 4 + q_row, -1)
    fourth = far_owner <= jnp.where(q_row == 4, asker, -1)
    allowed = jnp.where(k_row < 4, third.astype(jnp.int32), fourth.astype(jnp.int32)) > 0
    stat_row = iota((32, 64), 0)
    stats = jnp.zeros((32, 64), F32)
    accs = []
    for pair in range(PAIRS):
        at = lanes_of(pair)
        vat = slice(WIDTH + pair * LANES, WIDTH + (pair + 1) * LANES)
        queries = split_heads(jnp.concatenate([qa_ref[:, at], qb_ref[:, at]], 0))
        scores = jnp.where(allowed, dot_nt(kf_ref[:, at], queries), NEG)
        peak = jnp.max(scores, axis=0, keepdims=True)
        weights = jnp.where(allowed, jnp.exp(scores - peak), 0.0)
        total = jnp.sum(weights, axis=0, keepdims=True)
        acc = lax.dot_general(
            weights.astype(BF16), kf_ref[:, vat], (((0,), (0,)), ((), ())), preferred_element_type=F32
        )
        accs.append(join_heads(acc).astype(BF16))
        for side in range(2):
            here = slice(64 * side, 64 * side + 64)
            stats = jnp.where(stat_row == 2 * pair + side, peak[:, here], stats)
            stats = jnp.where(stat_row == STAT + 2 * pair + side, total[:, here], stats)
    high = stats.astype(BF16).astype(F32)
    mid = (stats - high).astype(BF16).astype(F32)
    low = stats - high - mid
    stats = jnp.concatenate([high, mid, low, jnp.zeros((32, 64), F32)], 0).T.astype(BF16)
    for number in range(8):
        to = device_of(number) & 7
        here = slice(number * 8, number * 8 + 8)
        for pair in range(PAIRS):
            out_ref[to, :, lanes_of(pair)] = accs[pair][here]
        out_ref[to, :, WIDTH:WIDTH + LANES] = stats[here]


def head_row(off_ref, level, shape, per_lane):
    lane = iota(shape, 1)
    lane = lane if per_lane else lane // HALF
    off = jnp.zeros(shape, jnp.int32)
    for head in range(HEADS):
        off = jnp.where(lane == head, off_ref[level, head], off)
    return off


def gathered(q_ref, parts, rows, allowed):
    stats = jnp.zeros((rows, LANES), F32)
    accs = []
    for pair in range(PAIRS):
        at = lanes_of(pair)
        vat = slice(WIDTH + pair * LANES, WIDTH + (pair + 1) * LANES)
        queries = split_heads(q_ref[:, at])
        scores = jnp.concatenate([dot_nt(queries, ref[:, at]) for ref in parts], 1)
        scores = jnp.where(allowed, scores, NEG)
        peak = jnp.max(scores, axis=1, keepdims=True)
        weights = jnp.exp(scores - peak)
        total = jnp.sum(weights, axis=1, keepdims=True)
        weights = weights.astype(BF16)
        acc = dot_nn(weights[:, 0:128], parts[0][:, vat]) + dot_nn(weights[:, 128:256], parts[1][:, vat])
        accs.append(join_heads(acc))
        stats = put_stats(stats, pair, peak, total)
    return accs, stats


def absorb(off_ref, level, accs, stats, acc_ref, out_ref):
    group = 4**level
    rows = TOK // group
    lane = iota((TOK, LANES), 1)
    tok = iota((TOK, LANES), 0)
    expand = jnp.where((iota((TOK, rows), 0) >> (2 * level)) == iota((TOK, rows), 1), 1.0, 0.0)
    spread = jnp.dot(expand, stats, precision=lax.Precision.HIGHEST, preferred_element_type=F32)
    kept = ((tok & (group - 1)) == head_row(off_ref, level, (1, LANES), True)) & (lane < HEADS)
    stat = acc_ref[:, WIDTH:WIDTH + LANES]
    peak0 = jnp.where(lane < HEADS, stat, 0.0)
    peak1 = jnp.where(kept, spread, NEG)
    best = jnp.maximum(peak0, peak1)
    share0 = jnp.where(lane < HEADS, jnp.exp(peak0 - best), 0.0)
    share1 = jnp.exp(peak1 - best)
    total = share0 * pltpu.roll(stat, LANES - STAT, 1) + share1 * pltpu.roll(spread, LANES - STAT, 1)
    out_ref[:, WIDTH:WIDTH + LANES] = jnp.where(
        lane < HEADS, best, pltpu.roll(jnp.where(lane < HEADS, total, 0.0), STAT, 1)
    )
    row_share = lax.dot_general(
        expand, share1, (((0,), (0,)), ((), ())), precision=lax.Precision.HIGHEST, preferred_element_type=F32
    )
    scale0 = over_lanes(share0)
    scale1 = over_lanes(row_share)
    twice = jnp.concatenate([expand.astype(BF16)] * 2, 1)
    for pair in range(PAIRS):
        at = lanes_of(pair)
        high, low = split2(accs[pair] * scale1[:, at])
        added = dot_nn(twice, jnp.concatenate([high, low], 0))
        side = iota((1, LANES), 1) >> 6
        off = jnp.where(side == 0, off_ref[level, 2 * pair], off_ref[level, 2 * pair + 1])
        added = jnp.where((iota((TOK, LANES), 0) & (group - 1)) == off, added, 0.0)
        out_ref[:, at] = scale0[:, at] * acc_ref[:, at] + added


def first_kernel(off_ref, pos_ref, q1_ref, a_ref, b_ref, acc_ref, out_ref):
    me = pos_ref[0]
    col = iota((1, TOK), 1)
    device = me ^ (((col >> 6) & 1) * 2) ^ (col >> 7)
    k_pos = (device & 3) * 64 + (col & 63)
    q_pos = (me & 3) * 64 + (iota((128, 1), 0) & 63)
    accs, stats = gathered(q1_ref, (a_ref, b_ref), 64, k_pos <= q_pos)
    absorb(off_ref, 1, accs, stats, acc_ref, out_ref)


def second_kernel(pos_ref, q2_ref, a_ref, b_ref, out_ref):
    me = pos_ref[0]
    col = iota((1, TOK), 1)
    block = (col >> 4) & 3
    device = me ^ ((block & 1) * 2) ^ ((block >> 1) * 6) ^ (((col >> 6) & 1) * 8) ^ (col >> 7)
    k_pos = (device & 15) * 16 + (col & 15)
    q_pos = (me & 15) * 16 + (iota((32, 1), 0) & 15)
    accs, stats = gathered(q2_ref, (a_ref, b_ref), 16, k_pos <= q_pos)
    for pair in range(PAIRS):
        out_ref[:, lanes_of(pair)] = accs[pair]
    out_ref[:, WIDTH:WIDTH + LANES] = stats


def split2(value):
    high = value.astype(BF16)
    return high, (value - high.astype(F32)).astype(BF16)


def over_lanes(coeff):
    high, low = split2(coeff)
    lane = iota((2 * LANES, WIDTH), 1) // HALF
    spread = jnp.where((iota((2 * LANES, WIDTH), 0) & (LANES - 1)) == lane, 1.0, 0.0).astype(BF16)
    return dot_nn(jnp.concatenate([high, low], 1), spread)


def final_kernel(off_ref, acc_ref, second_ref, ret_ref, out_ref):
    lane = iota((8, LANES), 1)
    parts = []
    for number in range(8):
        stats = ret_ref[number, :, WIDTH:WIDTH + LANES].astype(F32)
        parts.append(stats + pltpu.roll(stats, 96, 1) + pltpu.roll(stats, 64, 1))
    peaks = [jnp.where(lane < HEADS, part, NEG) for part in parts]
    peak = functools.reduce(jnp.maximum, peaks)
    factors = [jnp.where(lane < HEADS, jnp.exp(part - peak), 0.0) for part in peaks]
    total = sum(factor * pltpu.roll(part, LANES - STAT, 1) for factor, part in zip(factors, parts))
    spread = over_lanes(jnp.concatenate(factors, 0))
    rows = sum(
        spread[8 * number:8 * number + 8] * ret_ref[number, :, 0:WIDTH].astype(F32) for number in range(8)
    )
    second = second_ref[:, WIDTH:WIDTH + LANES]
    rows = jnp.concatenate([second_ref[:, 0:WIDTH], rows], 0)
    peak = jnp.concatenate([second, peak], 0)
    total = jnp.concatenate([pltpu.roll(second, LANES - STAT, 1), total], 0)

    def expanded(value, level):
        first = (0, 16, 20)[level - 2]
        group = 4**level
        pieces = [jnp.broadcast_to(value[first + r:first + r + 1], (group, LANES)) for r in range(TOK // group)]
        return jnp.concatenate(pieces, 0)

    lane = iota((TOK, LANES), 1)
    tok = iota((TOK, LANES), 0)
    stat = acc_ref[:, WIDTH:WIDTH + LANES]
    level_peaks = [jnp.where(lane < HEADS, stat, 0.0)]
    level_totals = [pltpu.roll(stat, LANES - STAT, 1)]
    for level in (2, 3, 4):
        kept = ((tok & (4**level - 1)) == head_row(off_ref, level, (1, LANES), True)) & (lane < HEADS)
        level_peaks.append(jnp.where(kept, expanded(peak, level), NEG))
        level_totals.append(expanded(total, level))
    best = functools.reduce(jnp.maximum, level_peaks)
    shares = [jnp.where(lane < HEADS, jnp.exp(value - best), 0.0) for value in level_peaks]
    denom = sum(share * value for share, value in zip(shares, level_totals))
    inverse = 1.0 / jnp.where(lane < HEADS, denom, 1.0)
    shares = [share * inverse for share in shares]
    row_shares = [jnp.sum(shares[1][16 * r:16 * r + 16], axis=0, keepdims=True) for r in range(16)]
    row_shares += [jnp.sum(shares[2][64 * r:64 * r + 64], axis=0, keepdims=True) for r in range(4)]
    row_shares += [jnp.sum(shares[3], axis=0, keepdims=True), jnp.zeros((3, LANES), F32)]
    rows = rows * over_lanes(jnp.concatenate(row_shares, 0))
    scale = over_lanes(shares[0])
    hits = [
        iota((4**level, WIDTH), 0) == head_row(off_ref, level, (1, WIDTH), False) for level in (2, 3, 4)
    ]
    for r in range(16):
        here = slice(16 * r, 16 * r + 16)
        inner = slice(16 * (r % 4), 16 * (r % 4) + 16)
        merged = scale[here] * acc_ref[here, 0:WIDTH]
        merged = merged + jnp.where(hits[0], rows[r:r + 1], 0.0)
        merged = merged + jnp.where(hits[1][inner], rows[16 + r // 4:17 + r // 4], 0.0)
        merged = merged + jnp.where(hits[2][here], rows[20:21], 0.0)
        out_ref[here, :] = merged.astype(BF16)


def shaped(rows, width, dtype):
    return jax.ShapeDtypeStruct((rows, width), dtype)


def traded(value, mask, count):
    return lax.ppermute(value, "ctx", [(source, source ^ mask) for source in range(count)])


def grown(value, mask, count):
    return jnp.concatenate([value, traded(value, mask, count)], 0)


def program(queries, keys, values, offsets):
    count = lax.axis_size("ctx")
    me = lax.axis_index("ctx").astype(jnp.int32).reshape(1)
    wide = 2 * WIDTH
    inputs = [pltpu.with_memory_space_constraint(a, pltpu.HBM) for a in (offsets, queries, keys, values)]
    q, k, v, q1, q2, kv1, early, third, fourth = call(
        select_kernel,
        [shaped(TOK, WIDTH, BF16)] * 3
        + [shaped(64, WIDTH, BF16), shaped(16, WIDTH, BF16), shaped(64, wide, BF16), shaped(24, wide, BF16),
           shaped(4, wide, BF16), shaped(1, wide, BF16)],
        [pl.BlockSpec(memory_space=pltpu.HBM)] * 4, 200_000_000, 2_000_000, 12,
        [pltpu.SMEM((5, HEADS), jnp.int32), pltpu.SemaphoreType.DMA((4,))],
    )(*inputs)
    fourth = grown(fourth, 192, count)
    fourth = grown(fourth, 64, count)
    far = jnp.broadcast_to(jnp.concatenate([third, fourth], 0)[None], (8, 8, wide))
    lines = [[first + step for step in range(0, 64, 8)] for first in range(count) if not first & 56]
    far = lax.all_to_all(far, "ctx", 0, 0, axis_index_groups=lines).reshape(64, wide)
    early = grown(early, 2, count)
    early = grown(early, 6, count).reshape(4, 24, wide)
    asked = early[:, 16:24, 0:WIDTH].reshape(32, WIDTH)
    asked_other = traded(asked, 1, count)
    kv1 = grown(kv1, 2, count)
    kv1_other = traded(kv1, 1, count)
    kv2 = grown(early[:, 0:16].reshape(64, wide), 8, count)
    kv2_other = traded(kv2, 1, count)
    total = shaped(TOK, WIDTH + LANES, F32)
    (acc,) = call(local_kernel, [total], [VMEM] * 3, 1_000_000_000, 3_000_000, 12)(q, k, v)
    (acc,) = call(first_kernel, [total], [SMEM, SMEM] + [VMEM] * 4, 600_000_000, 2_000_000, 16)(
        offsets, me, q1, kv1, kv1_other, acc
    )
    (partial,) = call(
        far_kernel, [jax.ShapeDtypeStruct((8, 8, WIDTH + LANES), BF16)], [SMEM] + [VMEM] * 3,
        200_000_000, 600_000, 12,
    )(me, asked, asked_other, far)
    groups = [list(range(first, first + 8)) for first in range(0, count, 8)]
    back = lax.all_to_all(partial, "ctx", 0, 0, axis_index_groups=groups)
    (second,) = call(
        second_kernel, [shaped(16, WIDTH + LANES, F32)], [SMEM] + [VMEM] * 3, 100_000_000, 900_000, 12
    )(me, q2, kv2, kv2_other)
    (merged,) = call(
        final_kernel, [shaped(TOK, WIDTH, BF16)], [SMEM] + [VMEM] * 3, 1_000_000_000, 3_000_000, 16
    )(offsets, acc, second, back)
    return merged


def solution(mesh):
    in_specs = (P("ctx", None), P("ctx", None), P("ctx", None), P())
    return jax.shard_map(program, mesh=mesh, in_specs=in_specs, out_specs=P("ctx", None), check_vma=False)
```

```python
import functools

import jax
import jax.numpy as jnp
from jax import lax
from jax.experimental import pallas as pl
from jax.experimental.pallas import tpu as pltpu
from jax.sharding import PartitionSpec as P

HEADS = 12
PAIRS = 6
LANES = 128
HALF = 64
TOK = 256
WIDTH = 768
NEG = -1e30
SCALE = 0.125
F32 = jnp.float32
BF16 = jnp.bfloat16
SEL = 96
STAT = 16
VMEM = pl.BlockSpec(memory_space=pltpu.VMEM)
SMEM = pl.BlockSpec(memory_space=pltpu.SMEM)


def iota(shape, dim):
    return lax.broadcasted_iota(jnp.int32, shape, dim)


def dot_nt(a, b):
    return lax.dot_general(a, b, (((1,), (1,)), ((), ())), preferred_element_type=F32)


def dot_nn(a, b):
    return jnp.dot(a, b, preferred_element_type=F32)


def lanes_of(pair):
    return slice(pair * LANES, (pair + 1) * LANES)


def split_heads(rows):
    low = iota(rows.shape, 1) < HALF
    zero = jnp.zeros_like(rows)
    return jnp.concatenate([jnp.where(low, rows, zero), jnp.where(low, zero, rows)], 0)


def join_heads(stacked):
    n = stacked.shape[0] // 2
    low = iota((n, LANES), 1) < HALF
    return jnp.where(low, stacked[:n], stacked[n:])


def put_stats(stats, pair, peak, total):
    n = stats.shape[0]
    lane = iota(stats.shape, 1)
    for side in range(2):
        head = 2 * pair + side
        stats = jnp.where(lane == head, peak[side * n:(side + 1) * n], stats)
        stats = jnp.where(lane == STAT + head, total[side * n:(side + 1) * n], stats)
    return stats


def call(body, outs, in_specs, flops, nbytes, grant, scratch=()):
    return pl.pallas_call(
        body,
        scratch_shapes=scratch,
        compiler_params=pltpu.CompilerParams(vmem_limit_bytes=grant << 20),
        out_shape=outs,
        in_specs=in_specs,
        out_specs=[VMEM] * len(outs),
        cost_estimate=pl.CostEstimate(flops=flops, bytes_accessed=nbytes, transcendentals=0),
    )


def select_kernel(
    off_hbm, q_hbm, k_hbm, v_hbm, q_ref, k_ref, v_ref, q1_ref, q2_ref, kv1_ref, early_ref, f3_ref, f4_ref, off_ref, sems
):
    pairs = ((off_hbm, off_ref), (q_hbm, q_ref), (k_hbm, k_ref), (v_hbm, v_ref))
    copies = [pltpu.make_async_copy(src, dst, sems.at[n]) for n, (src, dst) in enumerate(pairs)]
    for copy in copies:
        copy.start()
    for copy in copies:
        copy.wait()
    row = iota((SEL, TOK), 0)
    tok = iota((SEL, TOK), 1)
    base = jnp.where(row < 64, row * 4, jnp.where(row < 80, (row - 64) * 16, (row - 80) * 64))
    base = jnp.where(row < 84, base, 0)
    early_ref[16:24, WIDTH:2 * WIDTH] = jnp.zeros((8, WIDTH), BF16)
    tile_row = iota((16, LANES), 0)
    tile = jnp.zeros((16, LANES), F32)
    for pair in range(PAIRS):
        picks = []
        for side in range(2):
            head = 2 * pair + side
            off = jnp.where(
                row < 64,
                off_ref[1, head],
                jnp.where(row < 80, off_ref[2, head], jnp.where(row < 84, off_ref[3, head], off_ref[4, head])),
            )
            hit = (tok == base + off) & (row < 85)
            picks.append(jnp.where(hit, 1.0, 0.0).astype(BF16))
        pick = jnp.concatenate(picks, 0)
        at = lanes_of(pair)
        after = slice(WIDTH + pair * LANES, WIDTH + (pair + 1) * LANES)
        rows = join_heads(dot_nn(pick, q_ref[:, at]) * SCALE).astype(BF16)
        q1_ref[:, at] = rows[0:64]
        q2_ref[:, at] = rows[64:80]
        early_ref[16:24, at] = rows[80:88]
        for ref, here, number in ((k_ref, at, pair), (v_ref, after, PAIRS + pair)):
            rows = join_heads(dot_nn(pick, ref[:, at]))
            tile = jnp.where(tile_row == number, rows[84:85], tile)
            rows = rows.astype(BF16)
            kv1_ref[:, here] = rows[0:64]
            early_ref[0:16, here] = rows[64:80]
            f3_ref[:, here] = rows[80:84]
    tile = tile.astype(BF16)
    for number in range(32):
        f4_ref[number] = tile


def local_kernel(q_ref, k_ref, v_ref, acc_ref):
    half = TOK // 2
    for part in range(2):
        keys = (part + 1) * half
        here = slice(part * half, keys)
        query = iota((2 * half, keys), 0) % half + part * half
        allowed = iota((2 * half, keys), 1) <= query
        stats = jnp.zeros((half, LANES), F32)
        for pair in range(PAIRS):
            at = lanes_of(pair)
            queries = split_heads(q_ref[here, at] * jnp.asarray(SCALE, BF16))
            scores = jnp.where(allowed, dot_nt(queries, k_ref[0:keys, at]), NEG)
            peak = jnp.max(scores, axis=1, keepdims=True)
            weights = jnp.exp(scores - peak)
            total = jnp.sum(weights, axis=1, keepdims=True)
            acc_ref[here, at] = join_heads(dot_nn(weights.astype(BF16), v_ref[0:keys, at]))
            stats = put_stats(stats, pair, peak, total)
        acc_ref[here, WIDTH:WIDTH + LANES] = stats


def far_kernel(pos_ref, qa_ref, qb_ref, ka_ref, kb_ref, k4_ref, out_ref, tiles_ref):
    me = pos_ref[0]

    def device_of(block):
        return me ^ ((block & 1) * 2) ^ (((block >> 1) & 1) * 6) ^ (block >> 2)

    col = iota((1, 128), 1) & 63
    asker = device_of(col >> 3)
    q_row = col & 7
    row = iota((64, 1), 0)
    owner = me ^ (((row >> 2) & 1) * 32) ^ (((row >> 3) & 1) * 16) ^ (((row >> 4) & 1) * 8)
    third = (owner & 63) * 4 + (row & 3) <= jnp.where(q_row < 4, (asker & 63) * 4 + q_row, -1)
    owner = ((row >> 3) & 3) * 64 + (row & 7) * 8 + (me & 7)
    fourth = owner <= jnp.where(q_row == 4, asker, -1)
    allowed = jnp.where(row < 32, third.astype(jnp.int32), fourth.astype(jnp.int32)) > 0
    tiles_ref[...] = k4_ref[...].astype(F32).reshape(512, LANES)
    stat_row = iota((32, 64), 0)
    stats = jnp.zeros((32, 64), F32)
    accs = []
    for pair in range(PAIRS):
        at = lanes_of(pair)
        vat = slice(WIDTH + pair * LANES, WIDTH + (pair + 1) * LANES)
        queries = split_heads(jnp.concatenate([qa_ref[:, at], qb_ref[:, at]], 0))
        keys = tiles_ref[pl.ds(pair, 32, stride=16), :].astype(BF16)
        keys = jnp.concatenate([ka_ref[:, at], kb_ref[:, at], keys], 0)
        values = tiles_ref[pl.ds(PAIRS + pair, 32, stride=16), :].astype(BF16)
        values = jnp.concatenate([ka_ref[:, vat], kb_ref[:, vat], values], 0)
        scores = jnp.where(allowed, dot_nt(keys, queries), NEG)
        peak = jnp.max(scores, axis=0, keepdims=True)
        weights = jnp.where(allowed, jnp.exp(scores - peak), 0.0)
        total = jnp.sum(weights, axis=0, keepdims=True)
        acc = lax.dot_general(
            weights.astype(BF16), values, (((0,), (0,)), ((), ())), preferred_element_type=F32
        )
        accs.append(join_heads(acc).astype(BF16))
        for side in range(2):
            here = slice(64 * side, 64 * side + 64)
            stats = jnp.where(stat_row == 2 * pair + side, peak[:, here], stats)
            stats = jnp.where(stat_row == STAT + 2 * pair + side, total[:, here], stats)
    high = stats.astype(BF16).astype(F32)
    mid = (stats - high).astype(BF16).astype(F32)
    low = stats - high - mid
    stats = jnp.concatenate([high, mid, low, jnp.zeros((32, 64), F32)], 0).T.astype(BF16)
    for number in range(8):
        to = device_of(number) & 7
        here = slice(number * 8, number * 8 + 8)
        for pair in range(PAIRS):
            out_ref[to, :, lanes_of(pair)] = accs[pair][here]
        out_ref[to, :, WIDTH:WIDTH + LANES] = stats[here]


def head_row(off_ref, level, shape, per_lane):
    lane = iota(shape, 1)
    lane = lane if per_lane else lane // HALF
    off = jnp.zeros(shape, jnp.int32)
    for head in range(HEADS):
        off = jnp.where(lane == head, off_ref[level, head], off)
    return off


def gathered(q_ref, parts, rows, allowed):
    stats = jnp.zeros((rows, LANES), F32)
    accs = []
    for pair in range(PAIRS):
        at = lanes_of(pair)
        vat = slice(WIDTH + pair * LANES, WIDTH + (pair + 1) * LANES)
        queries = split_heads(q_ref[:, at])
        scores = jnp.concatenate([dot_nt(queries, ref[:, at]) for ref in parts], 1)
        scores = jnp.where(allowed, scores, NEG)
        peak = jnp.max(scores, axis=1, keepdims=True)
        weights = jnp.exp(scores - peak)
        total = jnp.sum(weights, axis=1, keepdims=True)
        weights = weights.astype(BF16)
        acc = dot_nn(weights[:, 0:128], parts[0][:, vat]) + dot_nn(weights[:, 128:256], parts[1][:, vat])
        accs.append(join_heads(acc))
        stats = put_stats(stats, pair, peak, total)
    return accs, stats


def absorb(off_ref, level, accs, stats, acc_ref, out_ref):
    group = 4**level
    rows = TOK // group
    lane = iota((TOK, LANES), 1)
    tok = iota((TOK, LANES), 0)
    expand = jnp.where((iota((TOK, rows), 0) >> (2 * level)) == iota((TOK, rows), 1), 1.0, 0.0)
    spread = jnp.dot(expand, stats, precision=lax.Precision.HIGHEST, preferred_element_type=F32)
    kept = ((tok & (group - 1)) == head_row(off_ref, level, (1, LANES), True)) & (lane < HEADS)
    stat = acc_ref[:, WIDTH:WIDTH + LANES]
    peak0 = jnp.where(lane < HEADS, stat, 0.0)
    peak1 = jnp.where(kept, spread, NEG)
    best = jnp.maximum(peak0, peak1)
    share0 = jnp.where(lane < HEADS, jnp.exp(peak0 - best), 0.0)
    share1 = jnp.exp(peak1 - best)
    total = share0 * pltpu.roll(stat, LANES - STAT, 1) + share1 * pltpu.roll(spread, LANES - STAT, 1)
    out_ref[:, WIDTH:WIDTH + LANES] = jnp.where(
        lane < HEADS, best, pltpu.roll(jnp.where(lane < HEADS, total, 0.0), STAT, 1)
    )
    row_share = lax.dot_general(
        expand, share1, (((0,), (0,)), ((), ())), precision=lax.Precision.HIGHEST, preferred_element_type=F32
    )
    scale0 = over_lanes(share0)
    scale1 = over_lanes(row_share)
    twice = jnp.concatenate([expand.astype(BF16)] * 2, 1)
    for pair in range(PAIRS):
        at = lanes_of(pair)
        high, low = split2(accs[pair] * scale1[:, at])
        added = dot_nn(twice, jnp.concatenate([high, low], 0))
        side = iota((1, LANES), 1) >> 6
        off = jnp.where(side == 0, off_ref[level, 2 * pair], off_ref[level, 2 * pair + 1])
        added = jnp.where((iota((TOK, LANES), 0) & (group - 1)) == off, added, 0.0)
        out_ref[:, at] = scale0[:, at] * acc_ref[:, at] + added


def first_kernel(off_ref, pos_ref, q1_ref, a_ref, b_ref, acc_ref, out_ref):
    me = pos_ref[0]
    col = iota((1, TOK), 1)
    device = me ^ (((col >> 6) & 1) * 2) ^ (col >> 7)
    k_pos = (device & 3) * 64 + (col & 63)
    q_pos = (me & 3) * 64 + (iota((128, 1), 0) & 63)
    accs, stats = gathered(q1_ref, (a_ref, b_ref), 64, k_pos <= q_pos)
    absorb(off_ref, 1, accs, stats, acc_ref, out_ref)


def second_kernel(pos_ref, q2_ref, a_ref, b_ref, out_ref):
    me = pos_ref[0]
    col = iota((1, TOK), 1)
    block = (col >> 4) & 3
    device = me ^ ((block & 1) * 2) ^ ((block >> 1) * 6) ^ (((col >> 6) & 1) * 8) ^ (col >> 7)
    k_pos = (device & 15) * 16 + (col & 15)
    q_pos = (me & 15) * 16 + (iota((32, 1), 0) & 15)
    accs, stats = gathered(q2_ref, (a_ref, b_ref), 16, k_pos <= q_pos)
    for pair in range(PAIRS):
        out_ref[:, lanes_of(pair)] = accs[pair]
    out_ref[:, WIDTH:WIDTH + LANES] = stats


def split2(value):
    high = value.astype(BF16)
    return high, (value - high.astype(F32)).astype(BF16)


def over_lanes(coeff):
    high, low = split2(coeff)
    lane = iota((2 * LANES, WIDTH), 1) // HALF
    spread = jnp.where((iota((2 * LANES, WIDTH), 0) & (LANES - 1)) == lane, 1.0, 0.0).astype(BF16)
    return dot_nn(jnp.concatenate([high, low], 1), spread)


def final_kernel(off_ref, acc_ref, second_ref, ret_ref, out_ref):
    lane = iota((8, LANES), 1)
    parts = []
    for number in range(8):
        stats = ret_ref[number, :, WIDTH:WIDTH + LANES].astype(F32)
        parts.append(stats + pltpu.roll(stats, 96, 1) + pltpu.roll(stats, 64, 1))
    peaks = [jnp.where(lane < HEADS, part, NEG) for part in parts]
    peak = functools.reduce(jnp.maximum, peaks)
    factors = [jnp.where(lane < HEADS, jnp.exp(part - peak), 0.0) for part in peaks]
    total = sum(factor * pltpu.roll(part, LANES - STAT, 1) for factor, part in zip(factors, parts))
    spread = over_lanes(jnp.concatenate(factors, 0))
    rows = sum(
        spread[8 * number:8 * number + 8] * ret_ref[number, :, 0:WIDTH].astype(F32) for number in range(8)
    )
    second = second_ref[:, WIDTH:WIDTH + LANES]
    rows = jnp.concatenate([second_ref[:, 0:WIDTH], rows], 0)
    peak = jnp.concatenate([second, peak], 0)
    total = jnp.concatenate([pltpu.roll(second, LANES - STAT, 1), total], 0)

    def expanded(value, level):
        first = (0, 16, 20)[level - 2]
        group = 4**level
        pieces = [jnp.broadcast_to(value[first + r:first + r + 1], (group, LANES)) for r in range(TOK // group)]
        return jnp.concatenate(pieces, 0)

    lane = iota((TOK, LANES), 1)
    tok = iota((TOK, LANES), 0)
    stat = acc_ref[:, WIDTH:WIDTH + LANES]
    level_peaks = [jnp.where(lane < HEADS, stat, 0.0)]
    level_totals = [pltpu.roll(stat, LANES - STAT, 1)]
    for level in (2, 3, 4):
        kept = ((tok & (4**level - 1)) == head_row(off_ref, level, (1, LANES), True)) & (lane < HEADS)
        level_peaks.append(jnp.where(kept, expanded(peak, level), NEG))
        level_totals.append(expanded(total, level))
    best = functools.reduce(jnp.maximum, level_peaks)
    shares = [jnp.where(lane < HEADS, jnp.exp(value - best), 0.0) for value in level_peaks]
    denom = sum(share * value for share, value in zip(shares, level_totals))
    inverse = 1.0 / jnp.where(lane < HEADS, denom, 1.0)
    shares = [share * inverse for share in shares]
    row_shares = [jnp.sum(shares[1][16 * r:16 * r + 16], axis=0, keepdims=True) for r in range(16)]
    row_shares += [jnp.sum(shares[2][64 * r:64 * r + 64], axis=0, keepdims=True) for r in range(4)]
    row_shares += [jnp.sum(shares[3], axis=0, keepdims=True), jnp.zeros((3, LANES), F32)]
    rows = rows * over_lanes(jnp.concatenate(row_shares, 0))
    scale = over_lanes(shares[0])
    hits = [
        iota((4**level, WIDTH), 0) == head_row(off_ref, level, (1, WIDTH), False) for level in (2, 3, 4)
    ]
    for r in range(16):
        here = slice(16 * r, 16 * r + 16)
        inner = slice(16 * (r % 4), 16 * (r % 4) + 16)
        merged = scale[here] * acc_ref[here, 0:WIDTH]
        merged = merged + jnp.where(hits[0], rows[r:r + 1], 0.0)
        merged = merged + jnp.where(hits[1][inner], rows[16 + r // 4:17 + r // 4], 0.0)
        merged = merged + jnp.where(hits[2][here], rows[20:21], 0.0)
        out_ref[here, :] = merged.astype(BF16)


def shaped(rows, width, dtype):
    return jax.ShapeDtypeStruct((rows, width), dtype)


def traded(value, mask, count):
    return lax.ppermute(value, "ctx", [(source, source ^ mask) for source in range(count)])


def grown(value, mask, count):
    return jnp.concatenate([value, traded(value, mask, count)], 0)


def program(queries, keys, values, offsets):
    count = lax.axis_size("ctx")
    me = lax.axis_index("ctx").astype(jnp.int32).reshape(1)
    wide = 2 * WIDTH
    inputs = [pltpu.with_memory_space_constraint(a, pltpu.HBM) for a in (offsets, queries, keys, values)]
    q, k, v, q1, q2, kv1, early, third, fourth = call(
        select_kernel,
        [shaped(TOK, WIDTH, BF16)] * 3
        + [shaped(64, WIDTH, BF16), shaped(16, WIDTH, BF16), shaped(64, wide, BF16), shaped(24, wide, BF16),
           shaped(4, wide, BF16), jax.ShapeDtypeStruct((32, 16, LANES), BF16)],
        [pl.BlockSpec(memory_space=pltpu.HBM)] * 4, 200_000_000, 2_000_000, 12,
        [pltpu.SMEM((5, HEADS), jnp.int32), pltpu.SemaphoreType.DMA((4,))],
    )(*inputs)
    planes = [
        [first + step * 64 + line * 8 for step in range(4) for line in range(8)] for first in range(8)
    ]
    fourth = lax.all_to_all(fourth, "ctx", 0, 0, axis_index_groups=planes)
    third = grown(third, 32, count)
    third = grown(third, 16, count)
    third_other = traded(third, 8, count)
    early = grown(early, 2, count)
    early = grown(early, 6, count).reshape(4, 24, wide)
    asked = early[:, 16:24, 0:WIDTH].reshape(32, WIDTH)
    asked_other = traded(asked, 1, count)
    kv1 = grown(kv1, 2, count)
    kv1_other = traded(kv1, 1, count)
    kv2 = grown(early[:, 0:16].reshape(64, wide), 8, count)
    kv2_other = traded(kv2, 1, count)
    total = shaped(TOK, WIDTH + LANES, F32)
    (acc,) = call(local_kernel, [total], [VMEM] * 3, 1_000_000_000, 3_000_000, 12)(q, k, v)
    (acc,) = call(first_kernel, [total], [SMEM, SMEM] + [VMEM] * 4, 600_000_000, 2_000_000, 16)(
        offsets, me, q1, kv1, kv1_other, acc
    )
    (partial,) = call(
        far_kernel, [jax.ShapeDtypeStruct((8, 8, WIDTH + LANES), BF16)], [SMEM] + [VMEM] * 5,
        200_000_000, 600_000, 12, [pltpu.VMEM((512, LANES), F32)],
    )(me, asked, asked_other, third, third_other, fourth)
    groups = [list(range(first, first + 8)) for first in range(0, count, 8)]
    back = lax.all_to_all(partial, "ctx", 0, 0, axis_index_groups=groups)
    (second,) = call(
        second_kernel, [shaped(16, WIDTH + LANES, F32)], [SMEM] + [VMEM] * 3, 100_000_000, 900_000, 12
    )(me, q2, kv2, kv2_other)
    (merged,) = call(
        final_kernel, [shaped(TOK, WIDTH, BF16)], [SMEM] + [VMEM] * 3, 1_000_000_000, 3_000_000, 16
    )(offsets, acc, second, back)
    return merged


def solution(mesh):
    in_specs = (P("ctx", None), P("ctx", None), P("ctx", None), P())
    return jax.shard_map(program, mesh=mesh, in_specs=in_specs, out_specs=P("ctx", None), check_vma=False)
```

```python
import functools

import jax
import jax.numpy as jnp
from jax import lax
from jax.experimental import pallas as pl
from jax.experimental.pallas import tpu as pltpu
from jax.sharding import PartitionSpec as P

HEADS = 12
PAIRS = 6
LANES = 128
HALF = 64
TOK = 256
WIDTH = 768
NEG = -1e30
SCALE = 0.125
F32 = jnp.float32
BF16 = jnp.bfloat16
SEL = 96
STAT = 16
VMEM = pl.BlockSpec(memory_space=pltpu.VMEM)
SMEM = pl.BlockSpec(memory_space=pltpu.SMEM)


def iota(shape, dim):
    return lax.broadcasted_iota(jnp.int32, shape, dim)


def dot_nt(a, b):
    return lax.dot_general(a, b, (((1,), (1,)), ((), ())), preferred_element_type=F32)


def dot_nn(a, b):
    return jnp.dot(a, b, preferred_element_type=F32)


def lanes_of(pair):
    return slice(pair * LANES, (pair + 1) * LANES)


def split_heads(rows):
    low = iota(rows.shape, 1) < HALF
    zero = jnp.zeros_like(rows)
    return jnp.concatenate([jnp.where(low, rows, zero), jnp.where(low, zero, rows)], 0)


def join_heads(stacked):
    n = stacked.shape[0] // 2
    low = iota((n, LANES), 1) < HALF
    return jnp.where(low, stacked[:n], stacked[n:])


def put_stats(stats, pair, peak, total):
    n = stats.shape[0]
    lane = iota(stats.shape, 1)
    for side in range(2):
        head = 2 * pair + side
        stats = jnp.where(lane == head, peak[side * n:(side + 1) * n], stats)
        stats = jnp.where(lane == STAT + head, total[side * n:(side + 1) * n], stats)
    return stats


def call(body, outs, in_specs, flops, nbytes, grant, scratch=(), space=pltpu.VMEM):
    return pl.pallas_call(
        body,
        scratch_shapes=scratch,
        compiler_params=pltpu.CompilerParams(vmem_limit_bytes=grant << 20),
        out_shape=outs,
        in_specs=in_specs,
        out_specs=[pl.BlockSpec(memory_space=space)] * len(outs),
        cost_estimate=pl.CostEstimate(flops=flops, bytes_accessed=nbytes, transcendentals=0),
    )


def select_kernel(
    off_hbm, q_hbm, k_hbm, v_hbm, q_ref, k_ref, v_ref, q1_ref, q2_ref, kv1_ref, early_ref, f3_ref, f4_ref, off_ref, pick_ref, sems
):
    pairs = ((off_hbm, off_ref), (q_hbm, q_ref), (k_hbm, k_ref), (v_hbm, v_ref))
    copies = [pltpu.make_async_copy(src, dst, sems.at[n]) for n, (src, dst) in enumerate(pairs)]
    for copy in copies:
        copy.start()
    row = iota((SEL, LANES), 0)
    tok = iota((SEL, LANES), 1)
    base = jnp.where(row < 64, row * 4, jnp.where(row < 80, (row - 64) * 16, (row - 80) * 64))
    base = jnp.where(row < 84, base, jnp.where(row < 85, 0, -4096))
    early_ref[16:24, WIDTH:2 * WIDTH] = jnp.zeros((8, WIDTH), BF16)
    copies[0].wait()
    for head in range(HEADS):
        off = jnp.where(
            row < 64,
            off_ref[1, head],
            jnp.where(row < 80, off_ref[2, head], jnp.where(row < 84, off_ref[3, head], off_ref[4, head])),
        )
        place = base + off
        pick = jnp.concatenate([jnp.where(tok == place, 1.0, 0.0), jnp.where(tok + LANES == place, 1.0, 0.0)], 1)
        pick_ref[SEL * head:SEL * head + SEL, :] = pick.astype(BF16)
    for copy in copies[1:]:
        copy.wait()
    for pair in range(PAIRS):
        pick = pick_ref[2 * SEL * pair:2 * SEL * pair + 2 * SEL, :]
        at = lanes_of(pair)
        after = slice(WIDTH + pair * LANES, WIDTH + (pair + 1) * LANES)
        rows = join_heads(dot_nn(pick, q_ref[:, at]) * SCALE).astype(BF16)
        q1_ref[:, at] = rows[0:64]
        q2_ref[:, at] = rows[64:80]
        early_ref[16:24, at] = rows[80:88]
        for ref, here in ((k_ref, at), (v_ref, after)):
            rows = join_heads(dot_nn(pick, ref[:, at])).astype(BF16)
            kv1_ref[:, here] = rows[0:64]
            early_ref[0:16, here] = rows[64:80]
            f3_ref[:, here] = rows[80:84]
            f4_ref[:, here] = rows[84:85]


def local_kernel(q_ref, k_ref, v_ref, acc_ref):
    half = TOK // 2
    for part in range(2):
        keys = (part + 1) * half
        here = slice(part * half, keys)
        query = iota((2 * half, keys), 0) % half + part * half
        allowed = iota((2 * half, keys), 1) <= query
        stats = jnp.zeros((half, LANES), F32)
        for pair in range(PAIRS):
            at = lanes_of(pair)
            queries = split_heads(q_ref[here, at] * jnp.asarray(SCALE, BF16))
            scores = jnp.where(allowed, dot_nt(queries, k_ref[0:keys, at]), NEG)
            peak = jnp.max(scores, axis=1, keepdims=True)
            weights = jnp.exp(scores - peak)
            total = jnp.sum(weights, axis=1, keepdims=True)
            acc_ref[here, at] = join_heads(dot_nn(weights.astype(BF16), v_ref[0:keys, at]))
            stats = put_stats(stats, pair, peak, total)
        acc_ref[here, WIDTH:WIDTH + LANES] = stats


def far_kernel(qa_ref, qb_ref, kf_ref, out_ref):
    me = lax.axis_index("ctx").astype(jnp.int32)

    def device_of(block):
        return me ^ ((block & 1) * 2) ^ (((block >> 1) & 1) * 6) ^ (block >> 2)

    col = iota((1, 128), 1) & 63
    asker = device_of(col >> 3)
    q_row = col & 7
    row = iota((64, 1), 0)
    k_row = row & 7
    owner = (me - (me & 56)) + (row >> 3) * 8
    far_owner = owner ^ ((k_row & 1) * 192) ^ (((k_row >> 1) & 1) * 64)
    third = (owner & 63) * 4 + k_row <= jnp.where(q_row < 4, (asker & 63) * 4 + q_row, -1)
    fourth = far_owner <= jnp.where(q_row == 4, asker, -1)
    allowed = jnp.where(k_row < 4, third.astype(jnp.int32), fourth.astype(jnp.int32)) > 0
    stat_row = iota((32, 64), 0)
    stats = jnp.zeros((32, 64), F32)
    accs = []
    for pair in range(PAIRS):
        at = lanes_of(pair)
        vat = slice(WIDTH + pair * LANES, WIDTH + (pair + 1) * LANES)
        queries = split_heads(jnp.concatenate([qa_ref[:, at], qb_ref[:, at]], 0))
        scores = jnp.where(allowed, dot_nt(kf_ref[:, at], queries), NEG)
        peak = jnp.max(scores, axis=0, keepdims=True)
        weights = jnp.where(allowed, jnp.exp(scores - peak), 0.0)
        total = jnp.sum(weights, axis=0, keepdims=True)
        acc = lax.dot_general(
            weights.astype(BF16), kf_ref[:, vat], (((0,), (0,)), ((), ())), preferred_element_type=F32
        )
        accs.append(join_heads(acc).astype(BF16))
        for side in range(2):
            here = slice(64 * side, 64 * side + 64)
            stats = jnp.where(stat_row == 2 * pair + side, peak[:, here], stats)
            stats = jnp.where(stat_row == STAT + 2 * pair + side, total[:, here], stats)
    high = stats.astype(BF16).astype(F32)
    mid = (stats - high).astype(BF16).astype(F32)
    low = stats - high - mid
    stats = jnp.concatenate([high, mid, low, jnp.zeros((32, 64), F32)], 0).T.astype(BF16)
    for number in range(8):
        to = device_of(number) & 7
        here = slice(number * 8, number * 8 + 8)
        for pair in range(PAIRS):
            out_ref[to, :, lanes_of(pair)] = accs[pair][here]
        out_ref[to, :, WIDTH:WIDTH + LANES] = stats[here]


def head_row(off_ref, level, shape, per_lane):
    lane = iota(shape, 1)
    lane = lane if per_lane else lane // HALF
    off = jnp.zeros(shape, jnp.int32)
    for head in range(HEADS):
        off = jnp.where(lane == head, off_ref[level, head], off)
    return off


def gathered(q_ref, parts, rows, allowed):
    stats = jnp.zeros((rows, LANES), F32)
    accs = []
    for pair in range(PAIRS):
        at = lanes_of(pair)
        vat = slice(WIDTH + pair * LANES, WIDTH + (pair + 1) * LANES)
        queries = split_heads(q_ref[:, at])
        scores = jnp.concatenate([dot_nt(queries, ref[:, at]) for ref in parts], 1)
        scores = jnp.where(allowed, scores, NEG)
        peak = jnp.max(scores, axis=1, keepdims=True)
        weights = jnp.exp(scores - peak)
        total = jnp.sum(weights, axis=1, keepdims=True)
        weights = weights.astype(BF16)
        acc = dot_nn(weights[:, 0:128], parts[0][:, vat]) + dot_nn(weights[:, 128:256], parts[1][:, vat])
        accs.append(join_heads(acc))
        stats = put_stats(stats, pair, peak, total)
    return accs, stats


def absorb(off_ref, level, accs, stats, acc_ref, out_ref):
    group = 4**level
    rows = TOK // group
    lane = iota((TOK, LANES), 1)
    tok = iota((TOK, LANES), 0)
    expand = jnp.where((iota((TOK, rows), 0) >> (2 * level)) == iota((TOK, rows), 1), 1.0, 0.0)
    spread = jnp.dot(expand, stats, precision=lax.Precision.HIGHEST, preferred_element_type=F32)
    kept = ((tok & (group - 1)) == head_row(off_ref, level, (1, LANES), True)) & (lane < HEADS)
    stat = acc_ref[:, WIDTH:WIDTH + LANES]
    peak0 = jnp.where(lane < HEADS, stat, 0.0)
    peak1 = jnp.where(kept, spread, NEG)
    best = jnp.maximum(peak0, peak1)
    share0 = jnp.where(lane < HEADS, jnp.exp(peak0 - best), 0.0)
    share1 = jnp.exp(peak1 - best)
    total = share0 * pltpu.roll(stat, LANES - STAT, 1) + share1 * pltpu.roll(spread, LANES - STAT, 1)
    out_ref[:, WIDTH:WIDTH + LANES] = jnp.where(
        lane < HEADS, best, pltpu.roll(jnp.where(lane < HEADS, total, 0.0), STAT, 1)
    )
    row_share = lax.dot_general(
        expand, share1, (((0,), (0,)), ((), ())), precision=lax.Precision.HIGHEST, preferred_element_type=F32
    )
    scale0 = over_lanes(share0)
    scale1 = over_lanes(row_share)
    twice = jnp.concatenate([expand.astype(BF16)] * 2, 1)
    for pair in range(PAIRS):
        at = lanes_of(pair)
        high, low = split2(accs[pair] * scale1[:, at])
        added = dot_nn(twice, jnp.concatenate([high, low], 0))
        side = iota((1, LANES), 1) >> 6
        off = jnp.where(side == 0, off_ref[level, 2 * pair], off_ref[level, 2 * pair + 1])
        added = jnp.where((iota((TOK, LANES), 0) & (group - 1)) == off, added, 0.0)
        out_ref[:, at] = scale0[:, at] * acc_ref[:, at] + added


def first_kernel(off_ref, q1_ref, a_ref, b_ref, acc_ref, out_ref, offs_ref):
    me = lax.axis_index("ctx").astype(jnp.int32)
    col = iota((1, TOK), 1)
    device = me ^ (((col >> 6) & 1) * 2) ^ (col >> 7)
    k_pos = (device & 3) * 64 + (col & 63)
    q_pos = (me & 3) * 64 + (iota((128, 1), 0) & 63)
    accs, stats = gathered(q1_ref, (a_ref, b_ref), 64, k_pos <= q_pos)
    absorb(off_ref, 1, accs, stats, acc_ref, out_ref)
    offs_ref[...] = jnp.zeros((8, WIDTH + LANES), jnp.int32)
    for level in (2, 3, 4):
        offs_ref[level:level + 1, 0:WIDTH] = head_row(off_ref, level, (1, WIDTH), False)
        offs_ref[level:level + 1, WIDTH:WIDTH + LANES] = head_row(off_ref, level, (1, LANES), True)


def second_kernel(q2_ref, a_ref, b_ref, out_ref):
    me = lax.axis_index("ctx").astype(jnp.int32)
    col = iota((1, TOK), 1)
    block = (col >> 4) & 3
    device = me ^ ((block & 1) * 2) ^ ((block >> 1) * 6) ^ (((col >> 6) & 1) * 8) ^ (col >> 7)
    k_pos = (device & 15) * 16 + (col & 15)
    q_pos = (me & 15) * 16 + (iota((32, 1), 0) & 15)
    accs, stats = gathered(q2_ref, (a_ref, b_ref), 16, k_pos <= q_pos)
    for pair in range(PAIRS):
        out_ref[:, lanes_of(pair)] = accs[pair]
    out_ref[:, WIDTH:WIDTH + LANES] = stats


def split2(value):
    high = value.astype(BF16)
    return high, (value - high.astype(F32)).astype(BF16)


def over_lanes(coeff):
    high, low = split2(coeff)
    lane = iota((2 * LANES, WIDTH), 1) // HALF
    spread = jnp.where((iota((2 * LANES, WIDTH), 0) & (LANES - 1)) == lane, 1.0, 0.0).astype(BF16)
    return dot_nn(jnp.concatenate([high, low], 1), spread)


def final_kernel(offs_ref, acc_ref, second_ref, ret_ref, out_hbm, out_ref, sems):
    lane = iota((8, LANES), 1)
    parts = []
    for number in range(8):
        stats = ret_ref[number, :, WIDTH:WIDTH + LANES].astype(F32)
        parts.append(stats + pltpu.roll(stats, 96, 1) + pltpu.roll(stats, 64, 1))
    peaks = [jnp.where(lane < HEADS, part, NEG) for part in parts]
    peak = functools.reduce(jnp.maximum, peaks)
    factors = [jnp.where(lane < HEADS, jnp.exp(part - peak), 0.0) for part in peaks]
    total = sum(factor * pltpu.roll(part, LANES - STAT, 1) for factor, part in zip(factors, parts))
    spread = over_lanes(jnp.concatenate(factors, 0))
    rows = sum(
        spread[8 * number:8 * number + 8] * ret_ref[number, :, 0:WIDTH].astype(F32) for number in range(8)
    )
    second = second_ref[:, WIDTH:WIDTH + LANES]
    rows = jnp.concatenate([second_ref[:, 0:WIDTH], rows], 0)
    peak = jnp.concatenate([second, peak], 0)
    total = jnp.concatenate([pltpu.roll(second, LANES - STAT, 1), total], 0)

    def expanded(value, level):
        first = (0, 16, 20)[level - 2]
        group = 4**level
        pieces = [jnp.broadcast_to(value[first + r:first + r + 1], (group, LANES)) for r in range(TOK // group)]
        return jnp.concatenate(pieces, 0)

    lane = iota((TOK, LANES), 1)
    tok = iota((TOK, LANES), 0)
    stat = acc_ref[:, WIDTH:WIDTH + LANES]
    level_peaks = [jnp.where(lane < HEADS, stat, 0.0)]
    level_totals = [pltpu.roll(stat, LANES - STAT, 1)]
    for level in (2, 3, 4):
        kept = ((tok & (4**level - 1)) == offs_ref[level:level + 1, WIDTH:WIDTH + LANES]) & (lane < HEADS)
        level_peaks.append(jnp.where(kept, expanded(peak, level), NEG))
        level_totals.append(expanded(total, level))
    best = functools.reduce(jnp.maximum, level_peaks)
    shares = [jnp.where(lane < HEADS, jnp.exp(value - best), 0.0) for value in level_peaks]
    denom = sum(share * value for share, value in zip(shares, level_totals))
    inverse = 1.0 / jnp.where(lane < HEADS, denom, 1.0)
    shares = [share * inverse for share in shares]
    row_shares = [jnp.sum(shares[1][16 * r:16 * r + 16], axis=0, keepdims=True) for r in range(16)]
    row_shares += [jnp.sum(shares[2][64 * r:64 * r + 64], axis=0, keepdims=True) for r in range(4)]
    row_shares += [jnp.sum(shares[3], axis=0, keepdims=True), jnp.zeros((3, LANES), F32)]
    rows = rows * over_lanes(jnp.concatenate(row_shares, 0))
    scale = over_lanes(shares[0])
    hits = [
        iota((4**level, WIDTH), 0) == offs_ref[level:level + 1, 0:WIDTH] for level in (2, 3, 4)
    ]
    copies = []
    for r in range(16):
        here = slice(16 * r, 16 * r + 16)
        inner = slice(16 * (r % 4), 16 * (r % 4) + 16)
        merged = scale[here] * acc_ref[here, 0:WIDTH]
        merged = merged + jnp.where(hits[0], rows[r:r + 1], 0.0)
        merged = merged + jnp.where(hits[1][inner], rows[16 + r // 4:17 + r // 4], 0.0)
        merged = merged + jnp.where(hits[2][here], rows[20:21], 0.0)
        out_ref[here, :] = merged.astype(BF16)
        if r % 4 == 3:
            done = slice(64 * (r // 4), 64 * (r // 4) + 64)
            copies.append(pltpu.make_async_copy(out_ref.at[done], out_hbm.at[done], sems.at[r // 4]))
            copies[-1].start()
    for copy in copies:
        copy.wait()


def shaped(rows, width, dtype):
    return jax.ShapeDtypeStruct((rows, width), dtype)


def traded(value, mask, count):
    return lax.ppermute(value, "ctx", [(source, source ^ mask) for source in range(count)])


def grown(value, mask, count):
    return jnp.concatenate([value, traded(value, mask, count)], 0)


def program(queries, keys, values, offsets):
    count = lax.axis_size("ctx")
    wide = 2 * WIDTH
    inputs = [pltpu.with_memory_space_constraint(a, pltpu.HBM) for a in (offsets, queries, keys, values)]
    q, k, v, q1, q2, kv1, early, third, fourth = call(
        select_kernel,
        [shaped(TOK, WIDTH, BF16)] * 3
        + [shaped(64, WIDTH, BF16), shaped(16, WIDTH, BF16), shaped(64, wide, BF16), shaped(24, wide, BF16),
           shaped(4, wide, BF16), shaped(1, wide, BF16)],
        [pl.BlockSpec(memory_space=pltpu.HBM)] * 4, 200_000_000, 2_000_000, 12,
        [pltpu.SMEM((5, HEADS), jnp.int32), pltpu.VMEM((HEADS * SEL, TOK), BF16), pltpu.SemaphoreType.DMA((4,))],
    )(*inputs)
    fourth = grown(fourth, 192, count)
    fourth = grown(fourth, 64, count)
    far = jnp.broadcast_to(jnp.concatenate([third, fourth], 0)[None], (8, 8, wide))
    lines = [[first + step for step in range(0, 64, 8)] for first in range(count) if not first & 56]
    far = lax.all_to_all(far, "ctx", 0, 0, axis_index_groups=lines).reshape(64, wide)
    early = grown(early, 2, count)
    early = grown(early, 6, count).reshape(4, 24, wide)
    asked = early[:, 16:24, 0:WIDTH].reshape(32, WIDTH)
    asked_other = traded(asked, 1, count)
    kv1 = grown(kv1, 2, count)
    kv1_other = traded(kv1, 1, count)
    kv2 = grown(early[:, 0:16].reshape(64, wide), 8, count)
    kv2_other = traded(kv2, 1, count)
    total = shaped(TOK, WIDTH + LANES, F32)
    (acc,) = call(local_kernel, [total], [VMEM] * 3, 1_000_000_000, 3_000_000, 12)(q, k, v)
    acc, places = call(
        first_kernel, [total, jax.ShapeDtypeStruct((8, WIDTH + LANES), jnp.int32)], [SMEM] + [VMEM] * 4,
        600_000_000, 2_000_000, 16,
    )(offsets, q1, kv1, kv1_other, acc)
    (partial,) = call(
        far_kernel, [jax.ShapeDtypeStruct((8, 8, WIDTH + LANES), BF16)], [VMEM] * 3,
        200_000_000, 600_000, 12,
    )(asked, asked_other, far)
    groups = [list(range(first, first + 8)) for first in range(0, count, 8)]
    back = lax.all_to_all(partial, "ctx", 0, 0, axis_index_groups=groups)
    (second,) = call(
        second_kernel, [shaped(16, WIDTH + LANES, F32)], [VMEM] * 3, 100_000_000, 900_000, 12
    )(q2, kv2, kv2_other)
    (merged,) = call(
        final_kernel, [shaped(TOK, WIDTH, BF16)], [VMEM] * 4, 1_000_000_000, 3_000_000, 16,
        [pltpu.VMEM((TOK, WIDTH), BF16), pltpu.SemaphoreType.DMA((4,))], pltpu.HBM,
    )(places, acc, second, back)
    return merged


def solution(mesh):
    in_specs = (P("ctx", None), P("ctx", None), P("ctx", None), P())
    return jax.shard_map(program, mesh=mesh, in_specs=in_specs, out_specs=P("ctx", None), check_vma=False)
```

```python
import functools

import jax
import jax.numpy as jnp
from jax import lax
from jax.experimental import pallas as pl
from jax.experimental.pallas import tpu as pltpu
from jax.sharding import PartitionSpec as P

HEADS = 12
PAIRS = 6
LANES = 128
HALF = 64
TOK = 256
WIDTH = 768
NEG = -1e30
SCALE = 0.125
F32 = jnp.float32
BF16 = jnp.bfloat16
SEL = 96
STAT = 16
VMEM = pl.BlockSpec(memory_space=pltpu.VMEM)
SMEM = pl.BlockSpec(memory_space=pltpu.SMEM)


def iota(shape, dim):
    return lax.broadcasted_iota(jnp.int32, shape, dim)


def dot_nt(a, b):
    return lax.dot_general(a, b, (((1,), (1,)), ((), ())), preferred_element_type=F32)


def dot_nn(a, b):
    return jnp.dot(a, b, preferred_element_type=F32)


def lanes_of(pair):
    return slice(pair * LANES, (pair + 1) * LANES)


def split_heads(rows):
    low = iota(rows.shape, 1) < HALF
    zero = jnp.zeros_like(rows)
    return jnp.concatenate([jnp.where(low, rows, zero), jnp.where(low, zero, rows)], 0)


def join_heads(stacked):
    n = stacked.shape[0] // 2
    low = iota((n, LANES), 1) < HALF
    return jnp.where(low, stacked[:n], stacked[n:])


def put_stats(stats, pair, peak, total):
    n = stats.shape[0]
    lane = iota(stats.shape, 1)
    for side in range(2):
        head = 2 * pair + side
        stats = jnp.where(lane == head, peak[side * n:(side + 1) * n], stats)
        stats = jnp.where(lane == STAT + head, total[side * n:(side + 1) * n], stats)
    return stats


def call(body, outs, in_specs, flops, nbytes, grant, scratch=(), space=pltpu.VMEM):
    return pl.pallas_call(
        body,
        scratch_shapes=scratch,
        compiler_params=pltpu.CompilerParams(vmem_limit_bytes=grant << 20),
        out_shape=outs,
        in_specs=in_specs,
        out_specs=[pl.BlockSpec(memory_space=space)] * len(outs),
        cost_estimate=pl.CostEstimate(flops=flops, bytes_accessed=nbytes, transcendentals=0),
    )


def head_row(off_ref, level, shape, per_lane):
    lane = iota(shape, 1)
    lane = lane if per_lane else lane // HALF
    off = jnp.zeros(shape, jnp.int32)
    for head in range(HEADS):
        off = jnp.where(lane == head, off_ref[level, head], off)
    return off


def select_kernel(
    off_hbm, q_hbm, k_hbm, v_hbm, q_ref, k_ref, v_ref, q1_ref, q2_ref, kv1_ref, early_ref, f3_ref, f4_ref, offs_ref, off_ref, pick_ref, sems
):
    pairs = ((off_hbm, off_ref), (q_hbm, q_ref), (k_hbm, k_ref), (v_hbm, v_ref))
    copies = [pltpu.make_async_copy(src, dst, sems.at[n]) for n, (src, dst) in enumerate(pairs)]
    for copy in copies:
        copy.start()
    row = iota((SEL, LANES), 0)
    tok = iota((SEL, LANES), 1)
    base = jnp.where(row < 64, row * 4, jnp.where(row < 80, (row - 64) * 16, (row - 80) * 64))
    base = jnp.where(row < 84, base, jnp.where(row < 85, 0, -4096))
    early_ref[16:24, WIDTH:2 * WIDTH] = jnp.zeros((8, WIDTH), BF16)
    copies[0].wait()
    for head in range(HEADS):
        off = jnp.where(
            row < 64,
            off_ref[1, head],
            jnp.where(row < 80, off_ref[2, head], jnp.where(row < 84, off_ref[3, head], off_ref[4, head])),
        )
        place = base + off
        pick = jnp.concatenate([jnp.where(tok == place, 1.0, 0.0), jnp.where(tok + LANES == place, 1.0, 0.0)], 1)
        pick_ref[SEL * head:SEL * head + SEL, :] = pick.astype(BF16)
    offs_ref[...] = jnp.zeros((8, WIDTH + LANES), jnp.int32)
    for level in range(1, 5):
        offs_ref[level:level + 1, 0:WIDTH] = head_row(off_ref, level, (1, WIDTH), False)
        offs_ref[level:level + 1, WIDTH:WIDTH + LANES] = head_row(off_ref, level, (1, LANES), True)
    for copy in copies[1:]:
        copy.wait()
    for pair in range(PAIRS):
        pick = pick_ref[2 * SEL * pair:2 * SEL * pair + 2 * SEL, :]
        at = lanes_of(pair)
        after = slice(WIDTH + pair * LANES, WIDTH + (pair + 1) * LANES)
        rows = join_heads(dot_nn(pick, q_ref[:, at]) * SCALE).astype(BF16)
        q1_ref[:, at] = rows[0:64]
        q2_ref[:, at] = rows[64:80]
        early_ref[16:24, at] = rows[80:88]
        for ref, here in ((k_ref, at), (v_ref, after)):
            rows = join_heads(dot_nn(pick, ref[:, at])).astype(BF16)
            kv1_ref[:, here] = rows[0:64]
            early_ref[0:16, here] = rows[64:80]
            f3_ref[:, here] = rows[80:84]
            f4_ref[:, here] = rows[84:85]


def local_kernel(q_ref, k_ref, v_ref, acc_ref):
    half = TOK // 2
    for part in range(2):
        keys = (part + 1) * half
        here = slice(part * half, keys)
        query = iota((2 * half, keys), 0) % half + part * half
        allowed = iota((2 * half, keys), 1) <= query
        stats = jnp.zeros((half, LANES), F32)
        for pair in range(PAIRS):
            at = lanes_of(pair)
            queries = split_heads(q_ref[here, at] * jnp.asarray(SCALE, BF16))
            scores = jnp.where(allowed, dot_nt(queries, k_ref[0:keys, at]), NEG)
            peak = jnp.max(scores, axis=1, keepdims=True)
            weights = jnp.exp(scores - peak)
            total = jnp.sum(weights, axis=1, keepdims=True)
            acc_ref[here, at] = join_heads(dot_nn(weights.astype(BF16), v_ref[0:keys, at]))
            stats = put_stats(stats, pair, peak, total)
        acc_ref[here, WIDTH:WIDTH + LANES] = stats


def far_kernel(qa_ref, qb_ref, kf_ref, out_ref):
    me = lax.axis_index("ctx").astype(jnp.int32)

    def device_of(block):
        return me ^ ((block & 1) * 2) ^ (((block >> 1) & 1) * 6) ^ (block >> 2)

    col = iota((1, 128), 1) & 63
    asker = device_of(col >> 3)
    q_row = col & 7
    row = iota((64, 1), 0)
    k_row = row & 7
    owner = (me - (me & 56)) + (row >> 3) * 8
    far_owner = owner ^ ((k_row & 1) * 192) ^ (((k_row >> 1) & 1) * 64)
    third = (owner & 63) * 4 + k_row <= jnp.where(q_row < 4, (asker & 63) * 4 + q_row, -1)
    fourth = far_owner <= jnp.where(q_row == 4, asker, -1)
    allowed = jnp.where(k_row < 4, third.astype(jnp.int32), fourth.astype(jnp.int32)) > 0
    stat_row = iota((32, 64), 0)
    stats = jnp.zeros((32, 64), F32)
    scores = []
    for pair in range(PAIRS):
        at = lanes_of(pair)
        queries = split_heads(jnp.concatenate([qa_ref[:, at], qb_ref[:, at]], 0))
        scores.append(dot_nt(kf_ref[:, at], queries))
    scores = [jnp.where(allowed, score, NEG) for score in scores]
    peaks = [jnp.max(score, axis=0, keepdims=True) for score in scores]
    weights = [jnp.where(allowed, jnp.exp(score - peak), 0.0) for score, peak in zip(scores, peaks)]
    accs = []
    for pair in range(PAIRS):
        vat = slice(WIDTH + pair * LANES, WIDTH + (pair + 1) * LANES)
        accs.append(
            lax.dot_general(
                weights[pair].astype(BF16), kf_ref[:, vat], (((0,), (0,)), ((), ())), preferred_element_type=F32
            )
        )
    totals = [jnp.sum(weight, axis=0, keepdims=True) for weight in weights]
    for pair in range(PAIRS):
        for side in range(2):
            here = slice(64 * side, 64 * side + 64)
            stats = jnp.where(stat_row == 2 * pair + side, peaks[pair][:, here], stats)
            stats = jnp.where(stat_row == STAT + 2 * pair + side, totals[pair][:, here], stats)
    accs = [join_heads(acc).astype(BF16) for acc in accs]
    high = stats.astype(BF16).astype(F32)
    mid = (stats - high).astype(BF16).astype(F32)
    low = stats - high - mid
    stats = jnp.concatenate([high, mid, low, jnp.zeros((32, 64), F32)], 0).T.astype(BF16)
    for number in range(8):
        to = device_of(number) & 7
        here = slice(number * 8, number * 8 + 8)
        for pair in range(PAIRS):
            out_ref[to, :, lanes_of(pair)] = accs[pair][here]
        out_ref[to, :, WIDTH:WIDTH + LANES] = stats[here]


def gathered(q_ref, parts, rows, allowed, together):
    stats = jnp.zeros((rows, LANES), F32)
    accs = []
    for first in range(0, PAIRS, together):
        pairs = range(first, first + together)
        scores = []
        for pair in pairs:
            queries = split_heads(q_ref[:, lanes_of(pair)])
            scores.append(jnp.concatenate([dot_nt(queries, ref[:, lanes_of(pair)]) for ref in parts], 1))
        scores = [jnp.where(allowed, score, NEG) for score in scores]
        peaks = [jnp.max(score, axis=1, keepdims=True) for score in scores]
        weights = [jnp.exp(score - peak) for score, peak in zip(scores, peaks)]
        totals = [jnp.sum(weight, axis=1, keepdims=True) for weight in weights]
        for pair, weight in zip(pairs, weights):
            vat = slice(WIDTH + pair * LANES, WIDTH + (pair + 1) * LANES)
            weight = weight.astype(BF16)
            acc = dot_nn(weight[:, 0:128], parts[0][:, vat]) + dot_nn(weight[:, 128:256], parts[1][:, vat])
            accs.append(join_heads(acc))
        for pair, peak, total in zip(pairs, peaks, totals):
            stats = put_stats(stats, pair, peak, total)
    return accs, stats


def absorb(offs_ref, level, accs, stats, acc_ref, out_ref):
    group = 4**level
    rows = TOK // group
    lane = iota((TOK, LANES), 1)
    tok = iota((TOK, LANES), 0)
    expand = jnp.where((iota((TOK, rows), 0) >> (2 * level)) == iota((TOK, rows), 1), 1.0, 0.0)
    spread = jnp.dot(expand, stats, precision=lax.Precision.HIGHEST, preferred_element_type=F32)
    kept = ((tok & (group - 1)) == offs_ref[level:level + 1, WIDTH:WIDTH + LANES]) & (lane < HEADS)
    stat = acc_ref[:, WIDTH:WIDTH + LANES]
    peak0 = jnp.where(lane < HEADS, stat, 0.0)
    peak1 = jnp.where(kept, spread, NEG)
    best = jnp.maximum(peak0, peak1)
    share0 = jnp.where(lane < HEADS, jnp.exp(peak0 - best), 0.0)
    share1 = jnp.exp(peak1 - best)
    total = share0 * pltpu.roll(stat, LANES - STAT, 1) + share1 * pltpu.roll(spread, LANES - STAT, 1)
    out_ref[:, WIDTH:WIDTH + LANES] = jnp.where(
        lane < HEADS, best, pltpu.roll(jnp.where(lane < HEADS, total, 0.0), STAT, 1)
    )
    row_share = lax.dot_general(
        expand, share1, (((0,), (0,)), ((), ())), precision=lax.Precision.HIGHEST, preferred_element_type=F32
    )
    scale0 = over_lanes(share0)
    scale1 = over_lanes(row_share)
    twice = jnp.concatenate([expand.astype(BF16)] * 2, 1)
    for pair in range(PAIRS):
        at = lanes_of(pair)
        high, low = split2(accs[pair] * scale1[:, at])
        added = dot_nn(twice, jnp.concatenate([high, low], 0))
        off = offs_ref[level:level + 1, at]
        added = jnp.where((iota((TOK, LANES), 0) & (group - 1)) == off, added, 0.0)
        out_ref[:, at] = scale0[:, at] * acc_ref[:, at] + added


def first_kernel(offs_ref, q1_ref, a_ref, b_ref, acc_ref, out_ref):
    me = lax.axis_index("ctx").astype(jnp.int32)
    col = iota((1, TOK), 1)
    device = me ^ (((col >> 6) & 1) * 2) ^ (col >> 7)
    k_pos = (device & 3) * 64 + (col & 63)
    q_pos = (me & 3) * 64 + (iota((128, 1), 0) & 63)
    accs, stats = gathered(q1_ref, (a_ref, b_ref), 64, k_pos <= q_pos, 2)
    absorb(offs_ref, 1, accs, stats, acc_ref, out_ref)


def second_kernel(q2_ref, a_ref, b_ref, out_ref):
    me = lax.axis_index("ctx").astype(jnp.int32)
    col = iota((1, TOK), 1)
    block = (col >> 4) & 3
    device = me ^ ((block & 1) * 2) ^ ((block >> 1) * 6) ^ (((col >> 6) & 1) * 8) ^ (col >> 7)
    k_pos = (device & 15) * 16 + (col & 15)
    q_pos = (me & 15) * 16 + (iota((32, 1), 0) & 15)
    accs, stats = gathered(q2_ref, (a_ref, b_ref), 16, k_pos <= q_pos, 6)
    for pair in range(PAIRS):
        out_ref[:, lanes_of(pair)] = accs[pair]
    out_ref[:, WIDTH:WIDTH + LANES] = stats


def split2(value):
    high = value.astype(BF16)
    return high, (value - high.astype(F32)).astype(BF16)


def over_lanes(coeff):
    high, low = split2(coeff)
    lane = iota((2 * LANES, WIDTH), 1) // HALF
    spread = jnp.where((iota((2 * LANES, WIDTH), 0) & (LANES - 1)) == lane, 1.0, 0.0).astype(BF16)
    return dot_nn(jnp.concatenate([high, low], 1), spread)


def final_kernel(offs_ref, acc_ref, second_ref, ret_ref, out_hbm, out_ref, sems):
    lane = iota((8, LANES), 1)
    parts = []
    for number in range(8):
        stats = ret_ref[number, :, WIDTH:WIDTH + LANES].astype(F32)
        parts.append(stats + pltpu.roll(stats, 96, 1) + pltpu.roll(stats, 64, 1))
    peaks = [jnp.where(lane < HEADS, part, NEG) for part in parts]
    peak = functools.reduce(jnp.maximum, peaks)
    factors = [jnp.where(lane < HEADS, jnp.exp(part - peak), 0.0) for part in peaks]
    total = sum(factor * pltpu.roll(part, LANES - STAT, 1) for factor, part in zip(factors, parts))
    spread = over_lanes(jnp.concatenate(factors, 0))
    rows = sum(
        spread[8 * number:8 * number + 8] * ret_ref[number, :, 0:WIDTH].astype(F32) for number in range(8)
    )
    second = second_ref[:, WIDTH:WIDTH + LANES]
    rows = jnp.concatenate([second_ref[:, 0:WIDTH], rows], 0)
    peak = jnp.concatenate([second, peak], 0)
    total = jnp.concatenate([pltpu.roll(second, LANES - STAT, 1), total], 0)

    def expanded(value, level):
        first = (0, 16, 20)[level - 2]
        group = 4**level
        pieces = [jnp.broadcast_to(value[first + r:first + r + 1], (group, LANES)) for r in range(TOK // group)]
        return jnp.concatenate(pieces, 0)

    lane = iota((TOK, LANES), 1)
    tok = iota((TOK, LANES), 0)
    stat = acc_ref[:, WIDTH:WIDTH + LANES]
    level_peaks = [jnp.where(lane < HEADS, stat, 0.0)]
    level_totals = [pltpu.roll(stat, LANES - STAT, 1)]
    for level in (2, 3, 4):
        kept = ((tok & (4**level - 1)) == offs_ref[level:level + 1, WIDTH:WIDTH + LANES]) & (lane < HEADS)
        level_peaks.append(jnp.where(kept, expanded(peak, level), NEG))
        level_totals.append(expanded(total, level))
    best = functools.reduce(jnp.maximum, level_peaks)
    shares = [jnp.where(lane < HEADS, jnp.exp(value - best), 0.0) for value in level_peaks]
    denom = sum(share * value for share, value in zip(shares, level_totals))
    inverse = 1.0 / jnp.where(lane < HEADS, denom, 1.0)
    shares = [share * inverse for share in shares]
    row_shares = [jnp.sum(shares[1][16 * r:16 * r + 16], axis=0, keepdims=True) for r in range(16)]
    row_shares += [jnp.sum(shares[2][64 * r:64 * r + 64], axis=0, keepdims=True) for r in range(4)]
    row_shares += [jnp.sum(shares[3], axis=0, keepdims=True), jnp.zeros((3, LANES), F32)]
    rows = rows * over_lanes(jnp.concatenate(row_shares, 0))
    scale = over_lanes(shares[0])
    hits = [
        iota((4**level, WIDTH), 0) == offs_ref[level:level + 1, 0:WIDTH] for level in (2, 3, 4)
    ]
    copies = []
    for r in range(16):
        here = slice(16 * r, 16 * r + 16)
        inner = slice(16 * (r % 4), 16 * (r % 4) + 16)
        merged = scale[here] * acc_ref[here, 0:WIDTH]
        merged = merged + jnp.where(hits[0], rows[r:r + 1], 0.0)
        merged = merged + jnp.where(hits[1][inner], rows[16 + r // 4:17 + r // 4], 0.0)
        merged = merged + jnp.where(hits[2][here], rows[20:21], 0.0)
        out_ref[here, :] = merged.astype(BF16)
        if r % 4 == 3:
            done = slice(64 * (r // 4), 64 * (r // 4) + 64)
            copies.append(pltpu.make_async_copy(out_ref.at[done], out_hbm.at[done], sems.at[r // 4]))
            copies[-1].start()
    for copy in copies:
        copy.wait()


def shaped(rows, width, dtype):
    return jax.ShapeDtypeStruct((rows, width), dtype)


def traded(value, mask, count):
    return lax.ppermute(value, "ctx", [(source, source ^ mask) for source in range(count)])


def grown(value, mask, count):
    other = traded(value, mask, count)
    return jnp.concatenate([value, other], 0)


def program(queries, keys, values, offsets):
    count = lax.axis_size("ctx")
    wide = 2 * WIDTH
    inputs = [pltpu.with_memory_space_constraint(a, pltpu.HBM) for a in (offsets, queries, keys, values)]
    q, k, v, q1, q2, kv1, early, third, fourth, places = call(
        select_kernel,
        [shaped(TOK, WIDTH, BF16)] * 3
        + [shaped(64, WIDTH, BF16), shaped(16, WIDTH, BF16), shaped(64, wide, BF16), shaped(24, wide, BF16),
           shaped(4, wide, BF16), shaped(1, wide, BF16), shaped(8, WIDTH + LANES, jnp.int32)],
        [pl.BlockSpec(memory_space=pltpu.HBM)] * 4, 200_000_000, 2_000_000, 12,
        [pltpu.SMEM((5, HEADS), jnp.int32), pltpu.VMEM((HEADS * SEL, TOK), BF16), pltpu.SemaphoreType.DMA((4,))],
    )(*inputs)
    fourth = grown(fourth, 192, count)
    fourth = grown(fourth, 64, count)
    far = jnp.broadcast_to(jnp.concatenate([third, fourth], 0)[None], (8, 8, wide))
    lines = [[first + step for step in range(0, 64, 8)] for first in range(count) if not first & 56]
    far = lax.all_to_all(far, "ctx", 0, 0, axis_index_groups=lines).reshape(64, wide)
    early = grown(early, 2, count)
    early = grown(early, 6, count).reshape(4, 24, wide)
    asked = early[:, 16:24, 0:WIDTH].reshape(32, WIDTH)
    asked_other = traded(asked, 1, count)
    kv1 = grown(kv1, 2, count)
    kv1_other = traded(kv1, 1, count)
    kv2 = grown(early[:, 0:16].reshape(64, wide), 8, count)
    kv2_other = traded(kv2, 1, count)
    total = shaped(TOK, WIDTH + LANES, F32)
    (acc,) = call(local_kernel, [total], [VMEM] * 3, 1_000_000_000, 3_000_000, 12)(q, k, v)
    (acc,) = call(first_kernel, [total], [VMEM] * 5, 600_000_000, 2_000_000, 16)(
        places, q1, kv1, kv1_other, acc
    )
    (partial,) = call(
        far_kernel, [jax.ShapeDtypeStruct((8, 8, WIDTH + LANES), BF16)], [VMEM] * 3,
        200_000_000, 600_000, 12,
    )(asked, asked_other, far)
    groups = [list(range(first, first + 8)) for first in range(0, count, 8)]
    back = lax.all_to_all(partial, "ctx", 0, 0, axis_index_groups=groups)
    (second,) = call(
        second_kernel, [shaped(16, WIDTH + LANES, F32)], [VMEM] * 3, 100_000_000, 900_000, 12
    )(q2, kv2, kv2_other)
    (merged,) = call(
        final_kernel, [shaped(TOK, WIDTH, BF16)], [VMEM] * 4, 1_000_000_000, 3_000_000, 16,
        [pltpu.VMEM((TOK, WIDTH), BF16), pltpu.SemaphoreType.DMA((4,))], pltpu.HBM,
    )(places, acc, second, back)
    return merged


def solution(mesh):
    in_specs = (P("ctx", None), P("ctx", None), P("ctx", None), P())
    return jax.shard_map(program, mesh=mesh, in_specs=in_specs, out_specs=P("ctx", None), check_vma=False)
```

```python
import functools

import jax
import jax.numpy as jnp
from jax import lax
from jax.experimental import pallas as pl
from jax.experimental.pallas import tpu as pltpu
from jax.sharding import PartitionSpec as P

HEADS = 12
PAIRS = 6
LANES = 128
HALF = 64
TOK = 256
WIDTH = 768
NEG = -1e30
SCALE = 0.125
F32 = jnp.float32
BF16 = jnp.bfloat16
SEL = 96
STAT = 16
VMEM = pl.BlockSpec(memory_space=pltpu.VMEM)
SMEM = pl.BlockSpec(memory_space=pltpu.SMEM)


def iota(shape, dim):
    return lax.broadcasted_iota(jnp.int32, shape, dim)


def dot_nt(a, b):
    return lax.dot_general(a, b, (((1,), (1,)), ((), ())), preferred_element_type=F32)


def dot_nn(a, b):
    return jnp.dot(a, b, preferred_element_type=F32)


def lanes_of(pair):
    return slice(pair * LANES, (pair + 1) * LANES)


def split_heads(rows):
    low = iota(rows.shape, 1) < HALF
    zero = jnp.zeros_like(rows)
    return jnp.concatenate([jnp.where(low, rows, zero), jnp.where(low, zero, rows)], 0)


def join_heads(stacked):
    n = stacked.shape[0] // 2
    low = iota((n, LANES), 1) < HALF
    return jnp.where(low, stacked[:n], stacked[n:])


def put_stats(stats, pair, peak, total):
    n = stats.shape[0]
    lane = iota(stats.shape, 1)
    for side in range(2):
        head = 2 * pair + side
        stats = jnp.where(lane == head, peak[side * n:(side + 1) * n], stats)
        stats = jnp.where(lane == STAT + head, total[side * n:(side + 1) * n], stats)
    return stats


def call(body, outs, in_specs, flops, nbytes, grant, scratch=(), space=pltpu.VMEM):
    return pl.pallas_call(
        body,
        scratch_shapes=scratch,
        compiler_params=pltpu.CompilerParams(vmem_limit_bytes=grant << 20),
        out_shape=outs,
        in_specs=in_specs,
        out_specs=[pl.BlockSpec(memory_space=space)] * len(outs),
        cost_estimate=pl.CostEstimate(flops=flops, bytes_accessed=nbytes, transcendentals=0),
    )


def head_row(off_ref, level, shape, per_lane):
    lane = iota(shape, 1)
    lane = lane if per_lane else lane // HALF
    off = jnp.zeros(shape, jnp.int32)
    for head in range(HEADS):
        off = jnp.where(lane == head, off_ref[level, head], off)
    return off


def start_copies(pairs, sems):
    copies = [pltpu.make_async_copy(src, dst, sems.at[n]) for n, (src, dst) in enumerate(pairs)]
    for copy in copies:
        copy.start()
    return copies


def one_hot(place):
    tok = iota(place.shape, 1)
    pick = jnp.concatenate([jnp.where(tok == place, 1.0, 0.0), jnp.where(tok + LANES == place, 1.0, 0.0)], 1)
    return pick.astype(BF16)


def far_select_kernel(off_hbm, k_hbm, v_hbm, k_ref, v_ref, f3_ref, f4_ref, offs_ref, off_ref, sems):
    copies = start_copies(((off_hbm, off_ref), (k_hbm, k_ref), (v_hbm, v_ref)), sems)
    row = iota((16, LANES), 0)
    copies[0].wait()
    picks = []
    for head in range(HEADS):
        place = jnp.where(row < 4, row * 64 + off_ref[3, head], jnp.where(row < 5, off_ref[4, head], -1))
        picks.append(one_hot(place))
    offs_ref[...] = jnp.zeros((8, WIDTH + LANES), jnp.int32)
    for level in range(1, 5):
        offs_ref[level:level + 1, 0:WIDTH] = head_row(off_ref, level, (1, WIDTH), False)
        offs_ref[level:level + 1, WIDTH:WIDTH + LANES] = head_row(off_ref, level, (1, LANES), True)
    for part, ref in enumerate((k_ref, v_ref)):
        copies[part + 1].wait()
        for pair in range(PAIRS):
            pick = jnp.concatenate(picks[2 * pair:2 * pair + 2], 0)
            rows = join_heads(dot_nn(pick, ref[:, lanes_of(pair)])).astype(BF16)
            here = slice(part * WIDTH + pair * LANES, part * WIDTH + (pair + 1) * LANES)
            f3_ref[:, here] = rows[0:4]
            f4_ref[:, here] = rows[4:5]


def near_select_kernel(
    off_hbm, q_hbm, k_ref, v_ref, q_ref, q1_ref, q2_ref, kv1_ref, early_ref, off_ref, pick_ref, sems
):
    copies = start_copies(((off_hbm, off_ref), (q_hbm, q_ref)), sems)
    row = iota((SEL, LANES), 0)
    base = jnp.where(row < 64, row * 4, jnp.where(row < 80, (row - 64) * 16, (row - 80) * 64))
    base = jnp.where(row < 84, base, jnp.where(row < 85, 0, -4096))
    early_ref[16:24, WIDTH:2 * WIDTH] = jnp.zeros((8, WIDTH), BF16)
    copies[0].wait()
    for head in range(HEADS):
        off = jnp.where(
            row < 64,
            off_ref[1, head],
            jnp.where(row < 80, off_ref[2, head], jnp.where(row < 84, off_ref[3, head], off_ref[4, head])),
        )
        pick_ref[SEL * head:SEL * head + SEL, :] = one_hot(base + off)
    copies[1].wait()
    for pair in range(PAIRS):
        pick = pick_ref[2 * SEL * pair:2 * SEL * pair + 2 * SEL, :]
        at = lanes_of(pair)
        after = slice(WIDTH + pair * LANES, WIDTH + (pair + 1) * LANES)
        rows = join_heads(dot_nn(pick, q_ref[:, at]) * SCALE).astype(BF16)
        q1_ref[:, at] = rows[0:64]
        q2_ref[:, at] = rows[64:80]
        early_ref[16:24, at] = rows[80:88]
        for ref, here in ((k_ref, at), (v_ref, after)):
            rows = join_heads(dot_nn(pick, ref[:, at])).astype(BF16)
            kv1_ref[:, here] = rows[0:64]
            early_ref[0:16, here] = rows[64:80]


def local_kernel(q_ref, k_ref, v_ref, acc_ref):
    half = TOK // 2
    for part in range(2):
        keys = (part + 1) * half
        here = slice(part * half, keys)
        query = iota((2 * half, keys), 0) % half + part * half
        allowed = iota((2 * half, keys), 1) <= query
        stats = jnp.zeros((half, LANES), F32)
        for pair in range(PAIRS):
            at = lanes_of(pair)
            queries = split_heads(q_ref[here, at] * jnp.asarray(SCALE, BF16))
            scores = jnp.where(allowed, dot_nt(queries, k_ref[0:keys, at]), NEG)
            peak = jnp.max(scores, axis=1, keepdims=True)
            weights = jnp.exp(scores - peak)
            total = jnp.sum(weights, axis=1, keepdims=True)
            acc_ref[here, at] = join_heads(dot_nn(weights.astype(BF16), v_ref[0:keys, at]))
            stats = put_stats(stats, pair, peak, total)
        acc_ref[here, WIDTH:WIDTH + LANES] = stats


def far_kernel(qa_ref, qb_ref, kf_ref, out_ref):
    me = lax.axis_index("ctx").astype(jnp.int32)

    def device_of(block):
        return me ^ ((block & 1) * 2) ^ (((block >> 1) & 1) * 6) ^ (block >> 2)

    col = iota((1, 128), 1) & 63
    asker = device_of(col >> 3)
    q_row = col & 7
    row = iota((64, 1), 0)
    k_row = row & 7
    owner = (me - (me & 56)) + (row >> 3) * 8
    far_owner = owner ^ ((k_row & 1) * 192) ^ (((k_row >> 1) & 1) * 64)
    third = (owner & 63) * 4 + k_row <= jnp.where(q_row < 4, (asker & 63) * 4 + q_row, -1)
    fourth = far_owner <= jnp.where(q_row == 4, asker, -1)
    allowed = jnp.where(k_row < 4, third.astype(jnp.int32), fourth.astype(jnp.int32)) > 0
    stat_row = iota((32, 64), 0)
    stats = jnp.zeros((32, 64), F32)
    scores = []
    for pair in range(PAIRS):
        at = lanes_of(pair)
        queries = split_heads(jnp.concatenate([qa_ref[:, at], qb_ref[:, at]], 0))
        scores.append(dot_nt(kf_ref[:, at], queries))
    scores = [jnp.where(allowed, score, NEG) for score in scores]
    peaks = [jnp.max(score, axis=0, keepdims=True) for score in scores]
    weights = [jnp.where(allowed, jnp.exp(score - peak), 0.0) for score, peak in zip(scores, peaks)]
    accs = []
    for pair in range(PAIRS):
        vat = slice(WIDTH + pair * LANES, WIDTH + (pair + 1) * LANES)
        accs.append(
            lax.dot_general(
                weights[pair].astype(BF16), kf_ref[:, vat], (((0,), (0,)), ((), ())), preferred_element_type=F32
            )
        )
    totals = [jnp.sum(weight, axis=0, keepdims=True) for weight in weights]
    for pair in range(PAIRS):
        for side in range(2):
            here = slice(64 * side, 64 * side + 64)
            stats = jnp.where(stat_row == 2 * pair + side, peaks[pair][:, here], stats)
            stats = jnp.where(stat_row == STAT + 2 * pair + side, totals[pair][:, here], stats)
    accs = [join_heads(acc).astype(BF16) for acc in accs]
    high = stats.astype(BF16).astype(F32)
    mid = (stats - high).astype(BF16).astype(F32)
    low = stats - high - mid
    stats = jnp.concatenate([high, mid, low, jnp.zeros((32, 64), F32)], 0).T.astype(BF16)
    for number in range(8):
        to = device_of(number) & 7
        here = slice(number * 8, number * 8 + 8)
        for pair in range(PAIRS):
            out_ref[to, :, lanes_of(pair)] = accs[pair][here]
        out_ref[to, :, WIDTH:WIDTH + LANES] = stats[here]


def gathered(q_ref, parts, rows, allowed, together):
    stats = jnp.zeros((rows, LANES), F32)
    accs = []
    for first in range(0, PAIRS, together):
        pairs = range(first, first + together)
        scores = []
        for pair in pairs:
            queries = split_heads(q_ref[:, lanes_of(pair)])
            scores.append(jnp.concatenate([dot_nt(queries, ref[:, lanes_of(pair)]) for ref in parts], 1))
        scores = [jnp.where(allowed, score, NEG) for score in scores]
        peaks = [jnp.max(score, axis=1, keepdims=True) for score in scores]
        weights = [jnp.exp(score - peak) for score, peak in zip(scores, peaks)]
        totals = [jnp.sum(weight, axis=1, keepdims=True) for weight in weights]
        for pair, weight in zip(pairs, weights):
            vat = slice(WIDTH + pair * LANES, WIDTH + (pair + 1) * LANES)
            weight = weight.astype(BF16)
            acc = dot_nn(weight[:, 0:128], parts[0][:, vat]) + dot_nn(weight[:, 128:256], parts[1][:, vat])
            accs.append(join_heads(acc))
        for pair, peak, total in zip(pairs, peaks, totals):
            stats = put_stats(stats, pair, peak, total)
    return accs, stats


def absorb(offs_ref, level, accs, stats, acc_ref, out_ref):
    group = 4**level
    rows = TOK // group
    lane = iota((TOK, LANES), 1)
    tok = iota((TOK, LANES), 0)
    expand = jnp.where((iota((TOK, rows), 0) >> (2 * level)) == iota((TOK, rows), 1), 1.0, 0.0)
    spread = jnp.dot(expand, stats, precision=lax.Precision.HIGHEST, preferred_element_type=F32)
    kept = ((tok & (group - 1)) == offs_ref[level:level + 1, WIDTH:WIDTH + LANES]) & (lane < HEADS)
    stat = acc_ref[:, WIDTH:WIDTH + LANES]
    peak0 = jnp.where(lane < HEADS, stat, 0.0)
    peak1 = jnp.where(kept, spread, NEG)
    best = jnp.maximum(peak0, peak1)
    share0 = jnp.where(lane < HEADS, jnp.exp(peak0 - best), 0.0)
    share1 = jnp.exp(peak1 - best)
    total = share0 * pltpu.roll(stat, LANES - STAT, 1) + share1 * pltpu.roll(spread, LANES - STAT, 1)
    out_ref[:, WIDTH:WIDTH + LANES] = jnp.where(
        lane < HEADS, best, pltpu.roll(jnp.where(lane < HEADS, total, 0.0), STAT, 1)
    )
    row_share = lax.dot_general(
        expand, share1, (((0,), (0,)), ((), ())), precision=lax.Precision.HIGHEST, preferred_element_type=F32
    )
    scale0 = over_lanes(share0)
    scale1 = over_lanes(row_share)
    twice = jnp.concatenate([expand.astype(BF16)] * 2, 1)
    for pair in range(PAIRS):
        at = lanes_of(pair)
        high, low = split2(accs[pair] * scale1[:, at])
        added = dot_nn(twice, jnp.concatenate([high, low], 0))
        off = offs_ref[level:level + 1, at]
        added = jnp.where((iota((TOK, LANES), 0) & (group - 1)) == off, added, 0.0)
        out_ref[:, at] = scale0[:, at] * acc_ref[:, at] + added


def first_kernel(offs_ref, q1_ref, a_ref, b_ref, acc_ref, out_ref):
    me = lax.axis_index("ctx").astype(jnp.int32)
    col = iota((1, TOK), 1)
    device = me ^ (((col >> 6) & 1) * 2) ^ (col >> 7)
    k_pos = (device & 3) * 64 + (col & 63)
    q_pos = (me & 3) * 64 + (iota((128, 1), 0) & 63)
    accs, stats = gathered(q1_ref, (a_ref, b_ref), 64, k_pos <= q_pos, 2)
    absorb(offs_ref, 1, accs, stats, acc_ref, out_ref)


def second_kernel(q2_ref, a_ref, b_ref, out_ref):
    me = lax.axis_index("ctx").astype(jnp.int32)
    col = iota((1, TOK), 1)
    block = (col >> 4) & 3
    device = me ^ ((block & 1) * 2) ^ ((block >> 1) * 6) ^ (((col >> 6) & 1) * 8) ^ (col >> 7)
    k_pos = (device & 15) * 16 + (col & 15)
    q_pos = (me & 15) * 16 + (iota((32, 1), 0) & 15)
    accs, stats = gathered(q2_ref, (a_ref, b_ref), 16, k_pos <= q_pos, 6)
    for pair in range(PAIRS):
        out_ref[:, lanes_of(pair)] = accs[pair]
    out_ref[:, WIDTH:WIDTH + LANES] = stats


def split2(value):
    high = value.astype(BF16)
    return high, (value - high.astype(F32)).astype(BF16)


def over_lanes(coeff):
    high, low = split2(coeff)
    lane = iota((2 * LANES, WIDTH), 1) // HALF
    spread = jnp.where((iota((2 * LANES, WIDTH), 0) & (LANES - 1)) == lane, 1.0, 0.0).astype(BF16)
    return dot_nn(jnp.concatenate([high, low], 1), spread)


def final_kernel(offs_ref, acc_ref, second_ref, ret_ref, out_hbm, out_ref, sems):
    lane = iota((8, LANES), 1)
    parts = []
    for number in range(8):
        stats = ret_ref[number, :, WIDTH:WIDTH + LANES].astype(F32)
        parts.append(stats + pltpu.roll(stats, 96, 1) + pltpu.roll(stats, 64, 1))
    peaks = [jnp.where(lane < HEADS, part, NEG) for part in parts]
    peak = functools.reduce(jnp.maximum, peaks)
    factors = [jnp.where(lane < HEADS, jnp.exp(part - peak), 0.0) for part in peaks]
    total = sum(factor * pltpu.roll(part, LANES - STAT, 1) for factor, part in zip(factors, parts))
    spread = over_lanes(jnp.concatenate(factors, 0))
    rows = sum(
        spread[8 * number:8 * number + 8] * ret_ref[number, :, 0:WIDTH].astype(F32) for number in range(8)
    )
    second = second_ref[:, WIDTH:WIDTH + LANES]
    rows = jnp.concatenate([second_ref[:, 0:WIDTH], rows], 0)
    peak = jnp.concatenate([second, peak], 0)
    total = jnp.concatenate([pltpu.roll(second, LANES - STAT, 1), total], 0)

    def expanded(value, level):
        first = (0, 16, 20)[level - 2]
        group = 4**level
        pieces = [jnp.broadcast_to(value[first + r:first + r + 1], (group, LANES)) for r in range(TOK // group)]
        return jnp.concatenate(pieces, 0)

    lane = iota((TOK, LANES), 1)
    tok = iota((TOK, LANES), 0)
    stat = acc_ref[:, WIDTH:WIDTH + LANES]
    level_peaks = [jnp.where(lane < HEADS, stat, 0.0)]
    level_totals = [pltpu.roll(stat, LANES - STAT, 1)]
    for level in (2, 3, 4):
        kept = ((tok & (4**level - 1)) == offs_ref[level:level + 1, WIDTH:WIDTH + LANES]) & (lane < HEADS)
        level_peaks.append(jnp.where(kept, expanded(peak, level), NEG))
        level_totals.append(expanded(total, level))
    best = functools.reduce(jnp.maximum, level_peaks)
    shares = [jnp.where(lane < HEADS, jnp.exp(value - best), 0.0) for value in level_peaks]
    denom = sum(share * value for share, value in zip(shares, level_totals))
    inverse = 1.0 / jnp.where(lane < HEADS, denom, 1.0)
    shares = [share * inverse for share in shares]
    row_shares = [jnp.sum(shares[1][16 * r:16 * r + 16], axis=0, keepdims=True) for r in range(16)]
    row_shares += [jnp.sum(shares[2][64 * r:64 * r + 64], axis=0, keepdims=True) for r in range(4)]
    row_shares += [jnp.sum(shares[3], axis=0, keepdims=True), jnp.zeros((3, LANES), F32)]
    rows = rows * over_lanes(jnp.concatenate(row_shares, 0))
    scale = over_lanes(shares[0])
    hits = [
        iota((4**level, WIDTH), 0) == offs_ref[level:level + 1, 0:WIDTH] for level in (2, 3, 4)
    ]
    copies = []
    for r in range(16):
        here = slice(16 * r, 16 * r + 16)
        inner = slice(16 * (r % 4), 16 * (r % 4) + 16)
        merged = scale[here] * acc_ref[here, 0:WIDTH]
        merged = merged + jnp.where(hits[0], rows[r:r + 1], 0.0)
        merged = merged + jnp.where(hits[1][inner], rows[16 + r // 4:17 + r // 4], 0.0)
        merged = merged + jnp.where(hits[2][here], rows[20:21], 0.0)
        out_ref[here, :] = merged.astype(BF16)
        if r % 4 == 3:
            done = slice(64 * (r // 4), 64 * (r // 4) + 64)
            copies.append(pltpu.make_async_copy(out_ref.at[done], out_hbm.at[done], sems.at[r // 4]))
            copies[-1].start()
    for copy in copies:
        copy.wait()


def shaped(rows, width, dtype):
    return jax.ShapeDtypeStruct((rows, width), dtype)


def traded(value, mask, count):
    return lax.ppermute(value, "ctx", [(source, source ^ mask) for source in range(count)])


def grown(value, mask, count):
    return jnp.concatenate([value, traded(value, mask, count)], 0)


def program(queries, keys, values, offsets):
    count = lax.axis_size("ctx")
    wide = 2 * WIDTH
    off, queries, keys, values = [
        pltpu.with_memory_space_constraint(a, pltpu.HBM) for a in (offsets, queries, keys, values)
    ]
    hbm = pl.BlockSpec(memory_space=pltpu.HBM)
    smem = pltpu.SMEM((5, HEADS), jnp.int32)
    k, v, third, fourth, places = call(
        far_select_kernel,
        [shaped(TOK, WIDTH, BF16)] * 2
        + [shaped(4, wide, BF16), shaped(1, wide, BF16), shaped(8, WIDTH + LANES, jnp.int32)],
        [hbm] * 3, 50_000_000, 1_000_000, 12, [smem, pltpu.SemaphoreType.DMA((3,))],
    )(off, keys, values)
    q, q1, q2, kv1, early = call(
        near_select_kernel,
        [shaped(TOK, WIDTH, BF16), shaped(64, WIDTH, BF16), shaped(16, WIDTH, BF16), shaped(64, wide, BF16),
         shaped(24, wide, BF16)],
        [hbm] * 2 + [VMEM] * 2, 150_000_000, 1_000_000, 12,
        [smem, pltpu.VMEM((HEADS * SEL, TOK), BF16), pltpu.SemaphoreType.DMA((2,))],
    )(off, queries, k, v)
    fourth = grown(fourth, 192, count)
    fourth = grown(fourth, 64, count)
    far = jnp.broadcast_to(jnp.concatenate([third, fourth], 0)[None], (8, 8, wide))
    lines = [[first + step for step in range(0, 64, 8)] for first in range(count) if not first & 56]
    far = lax.all_to_all(far, "ctx", 0, 0, axis_index_groups=lines).reshape(64, wide)
    early = grown(early, 2, count)
    early = grown(early, 6, count).reshape(4, 24, wide)
    asked = early[:, 16:24, 0:WIDTH].reshape(32, WIDTH)
    asked_other = traded(asked, 1, count)
    kv1 = grown(kv1, 2, count)
    kv1_other = traded(kv1, 1, count)
    kv2 = grown(early[:, 0:16].reshape(64, wide), 8, count)
    kv2_other = traded(kv2, 1, count)
    total = shaped(TOK, WIDTH + LANES, F32)
    (acc,) = call(local_kernel, [total], [VMEM] * 3, 1_000_000_000, 3_000_000, 12)(q, k, v)
    (acc,) = call(first_kernel, [total], [VMEM] * 5, 600_000_000, 2_000_000, 16)(
        places, q1, kv1, kv1_other, acc
    )
    (partial,) = call(
        far_kernel, [jax.ShapeDtypeStruct((8, 8, WIDTH + LANES), BF16)], [VMEM] * 3,
        200_000_000, 600_000, 12,
    )(asked, asked_other, far)
    groups = [list(range(first, first + 8)) for first in range(0, count, 8)]
    back = lax.all_to_all(partial, "ctx", 0, 0, axis_index_groups=groups)
    (second,) = call(
        second_kernel, [shaped(16, WIDTH + LANES, F32)], [VMEM] * 3, 100_000_000, 900_000, 12
    )(q2, kv2, kv2_other)
    (merged,) = call(
        final_kernel, [shaped(TOK, WIDTH, BF16)], [VMEM] * 4, 1_000_000_000, 3_000_000, 16,
        [pltpu.VMEM((TOK, WIDTH), BF16), pltpu.SemaphoreType.DMA((4,))], pltpu.HBM,
    )(places, acc, second, back)
    return merged


def solution(mesh):
    in_specs = (P("ctx", None), P("ctx", None), P("ctx", None), P())
    return jax.shard_map(program, mesh=mesh, in_specs=in_specs, out_specs=P("ctx", None), check_vma=False)
```
